512 devices in a mesh: seq: 64 (over z_lo, y, core), dp: 8 (over z_hi, x).
Axes of the slice: x: 4, y: 4, z: 16 (z_hi: 2, z_lo: 8; z = z_hi * 8 + z_lo), core: 2. Of those that a mesh axis runs over, the one named last changes fastest.
Arguments:
- q_raw: bfloat16 [8, 16384, 1024], P('dp', 'seq'), may hold values from -400 to 400
- k_raw: bfloat16 [8, 16384, 512], P('dp', 'seq'), may hold values from -400 to 400
- values: bfloat16 [8, 16384, 512], P('dp', 'seq'), may hold values from -6 to 6
- grad_out: bfloat16 [8, 16384, 1024], P('dp', 'seq'), may hold values from -80 to 80
- q_gain: float32 [256], replicated, may hold values from 0.5 to 7
- k_gain: float32 [256], replicated, may hold values from 0.5 to 7
Outputs:
- grad_q_raw: bfloat16 [8, 16384, 1024], P('dp', 'seq')
- grad_k_raw: bfloat16 [8, 16384, 512], P('dp', 'seq')
- grad_values: bfloat16 [8, 16384, 512], P('dp', 'seq')
- grad_q_gain: float32 [256], replicated
- grad_k_gain: float32 [256], replicated
The draws below stay inside these ranges and needn't reach their ends.
All inputs are finite; a program needn't handle non-finite values.
Results may differ from the reference program's by a relative error of at most 0.029.
The reference program's roundings to bfloat16 on the way (of `q_rot`, `k_rot`, `weights_b` and `dscores`) count: a program that leaves them out, or rounds other values in their place, can miss the bound.
Values may be sent and summed in bfloat16 or wider, within the bound.
A program may use at most 128 MiB of HBM per device.

```python
import math
import jax
import jax.numpy as jnp
from jax import lax

QH = 4
KVH = 2
HD = 256
WINDOW = 1024
TOK_DEV = 256
SEQLEN = 16384
BATCH = 8


def base_rows(key, head_count):
    shape = (BATCH, SEQLEN, head_count, HD)
    row_scale = jnp.exp(jax.random.uniform(jax.random.fold_in(key, 1), (BATCH, SEQLEN, head_count, 1), jnp.float32, 0.0, math.log(10.0)))
    entries = jax.random.truncated_normal(jax.random.fold_in(key, 2), -4.0, 4.0, shape, jnp.float32)
    col_scale = jnp.exp(jax.random.uniform(jax.random.fold_in(key, 3), (HD,), jnp.float32, 0.0, math.log(10.0)))
    return entries * row_scale * col_scale


def draw_q_raw(key, part):
    rows = base_rows(jax.random.fold_in(key, 101), QH)
    return rows.reshape(BATCH, SEQLEN, QH * HD).astype(jnp.bfloat16)


def draw_k_raw(key, part):
    rows = base_rows(jax.random.fold_in(key, 202), KVH)
    return rows.reshape(BATCH, SEQLEN, KVH * HD).astype(jnp.bfloat16)


def draw_grad_out(key, part):
    own_key = jax.random.fold_in(key, 303)
    shape = (BATCH, SEQLEN, QH, HD)
    positions = jnp.arange(SEQLEN, dtype=jnp.float32)
    ramp = jnp.exp(math.log(3.0) * positions / SEQLEN)
    entries = jax.random.truncated_normal(jax.random.fold_in(own_key, 1), -4.0, 4.0, shape, jnp.float32)
    row_scale = jnp.exp(jax.random.uniform(jax.random.fold_in(own_key, 3), (BATCH, SEQLEN, QH, 1), jnp.float32, 0.0, math.log(3.0)))
    rows = entries * row_scale * ramp[None, :, None, None]
    return rows.reshape(BATCH, SEQLEN, QH * HD).astype(jnp.bfloat16)


def draw_gain(key):
    gains = jnp.exp(jax.random.uniform(jax.random.fold_in(key, 1), (HD,), jnp.float32, math.log(0.5), math.log(2.0)))
    return gains


def draw_q_gain(key, part):
    return draw_gain(jax.random.fold_in(key, 404))


def draw_k_gain(key, part):
    return draw_gain(jax.random.fold_in(key, 505))


def block_scale(stream_key, shape, split, least, high):
    def one(dim, shards_of):
        steps = jax.random.uniform(jax.random.fold_in(jax.random.fold_in(stream_key, 6), dim), (shards_of,), jnp.float32, least / len(split), high / len(split))
        return jnp.repeat(jnp.exp(steps), shape[dim] // shards_of).reshape((-1,) + (1,) * (len(shape) - dim - 1))

    gain = one(*split[0])
    for cut in split[1:]:
        gain = gain * one(*cut)
    return gain


def bell_draw(stream_key, shape, spread, limit, cuts=(), held_as=jnp.bfloat16):
    values = jax.random.normal(stream_key, shape, jnp.float32) * spread
    if len(cuts) > 0:
        values = block_scale(stream_key, shape, cuts, -0.22, 0.18) * values
    return jnp.clip(values, min=-limit, max=limit).astype(held_as)


def setup_inputs(seed: int = 0) -> dict:
    arg_keys = jax.random.split(jax.random.key(seed), 7)
    q_raw = draw_q_raw(jax.random.fold_in(arg_keys[6], 71), 0)
    k_raw = draw_k_raw(jax.random.fold_in(arg_keys[6], 71), 0)
    values = bell_draw(arg_keys[2], (BATCH, SEQLEN, KVH * HD), 1.0, 6.0, ((0, 8), (1, 64)))
    grad_out = draw_grad_out(jax.random.fold_in(arg_keys[6], 71), 0)
    q_gain = draw_q_gain(jax.random.fold_in(arg_keys[6], 71), 0)
    k_gain = draw_k_gain(jax.random.fold_in(arg_keys[6], 71), 0)
    return dict(q_raw=q_raw, k_raw=k_raw, values=values, grad_out=grad_out, q_gain=q_gain, k_gain=k_gain)


EPS = 1e-06
ROPE_BASE = 10000.0
MASKED = -1e+30

def rope_tables(positions):
    half_size = HD // 2
    freqs = jnp.power(ROPE_BASE, -(2.0 * jnp.arange(half_size, dtype=jnp.float32)) / HD)
    angles = positions.astype(jnp.float32)[:, None] * freqs[None, :]
    return (jnp.cos(angles), jnp.sin(angles))

def norm_rope(raw_in, gain_in, cosine, sine, head_count):
    row_count = raw_in.shape[0]
    inputs = raw_in.reshape(row_count, head_count, HD)
    inverse = lax.rsqrt(lax.optimization_barrier(jnp.mean(inputs * inputs, axis=-1, keepdims=True)) + EPS)
    scaled = inputs * inverse * gain_in
    half_size = HD // 2
    lower = scaled[..., :half_size]
    upper = scaled[..., half_size:]
    cos_rows = cosine[:, None, :]
    sin_rows = sine[:, None, :]
    turned = jnp.concatenate([lower * cos_rows - upper * sin_rows, upper * cos_rows + lower * sin_rows], axis=-1)
    return turned.reshape(row_count, head_count * HD)

def round_trip(block):
    return lax.optimization_barrier(block.astype(jnp.bfloat16)).astype(jnp.float32)

def attention_block(q_blk, k_win, v_win, do_blk, block_start):
    row_count = q_blk.shape[0]
    key_span = k_win.shape[0]
    group_size = QH // KVH
    q_heads = q_blk.astype(jnp.float32).reshape(row_count, KVH, group_size, HD)
    k_heads = k_win.astype(jnp.float32).reshape(key_span, KVH, HD)
    v_heads = v_win.astype(jnp.float32).reshape(key_span, KVH, HD)
    do_heads = do_blk.astype(jnp.float32).reshape(row_count, KVH, group_size, HD)
    query_idx = jnp.arange(row_count, dtype=jnp.int32)[:, None]
    key_idx = jnp.arange(key_span, dtype=jnp.int32)[None, :]
    distance = query_idx + WINDOW - key_idx
    visible = (distance >= 0) & (distance < WINDOW) & (key_idx >= WINDOW - block_start)
    score_scale = HD ** (-0.5)
    scores = jnp.einsum('tkgd,skd->kgts', q_heads, k_heads) * score_scale
    scores = jnp.where(visible, scores, MASKED)
    row_top = lax.optimization_barrier(jnp.max(scores, axis=-1, keepdims=True))
    row_total = jnp.log(lax.optimization_barrier(jnp.sum(jnp.exp(scores - row_top), axis=-1, keepdims=True))) + row_top
    weights = jnp.exp(scores - row_total)
    weights_b = lax.optimization_barrier(weights.astype(jnp.bfloat16))
    dweights = jnp.einsum('tkgd,skd->kgts', do_heads, v_heads)
    row_delta = lax.optimization_barrier(jnp.sum(weights * dweights, axis=-1, keepdims=True))
    dscores = lax.optimization_barrier((weights * (dweights - row_delta) * score_scale).astype(jnp.bfloat16))
    dscores_f = dscores.astype(jnp.float32)
    grad_q = jnp.einsum('kgts,skd->tkgd', dscores_f, k_heads).reshape(row_count, QH * HD)
    grad_k = jnp.einsum('kgts,tkgd->skd', dscores_f, q_heads).reshape(key_span, KVH * HD)
    grad_v = jnp.einsum('kgts,tkgd->skd', weights_b.astype(jnp.float32), do_heads).reshape(key_span, KVH * HD)
    grad_k = jnp.concatenate([round_trip(grad_k[:WINDOW]), grad_k[WINDOW:]], axis=0)
    grad_v = jnp.concatenate([round_trip(grad_v[:WINDOW]), grad_v[WINDOW:]], axis=0)
    return (grad_q, grad_k, grad_v)

def one_sequence(q_raw, k_raw, values, grad_out, q_gain, k_gain):
    length = q_raw.shape[0]
    positions = jnp.arange(length, dtype=jnp.int32)
    cosine, sine = rope_tables(positions)
    q_rot32, q_back = jax.vjp(lambda raw_in, gain_in: norm_rope(raw_in, gain_in, cosine, sine, QH), q_raw.astype(jnp.float32), q_gain)
    k_rot32, k_back = jax.vjp(lambda raw_in, gain_in: norm_rope(raw_in, gain_in, cosine, sine, KVH), k_raw.astype(jnp.float32), k_gain)
    q_rot = q_rot32.astype(jnp.bfloat16)
    k_rot = k_rot32.astype(jnp.bfloat16)
    key_width = KVH * HD
    k_pad = jnp.concatenate([jnp.zeros((WINDOW, key_width), jnp.bfloat16), k_rot], axis=0)
    v_pad = jnp.concatenate([jnp.zeros((WINDOW, key_width), jnp.bfloat16), values], axis=0)
    blocks = length // TOK_DEV
    key_span = WINDOW + TOK_DEV

    def advance(state_pair, block_idx):
        dk_acc, dv_acc = state_pair
        block_start = block_idx * TOK_DEV
        q_blk = lax.dynamic_slice_in_dim(q_rot, block_start, TOK_DEV, 0)
        do_blk = lax.dynamic_slice_in_dim(grad_out, block_start, TOK_DEV, 0)
        k_win = lax.dynamic_slice_in_dim(k_pad, block_start, key_span, 0)
        v_win = lax.dynamic_slice_in_dim(v_pad, block_start, key_span, 0)
        grad_q, grad_k, grad_v = attention_block(q_blk, k_win, v_win, do_blk, block_start)
        dk_acc = lax.dynamic_update_slice_in_dim(dk_acc, lax.dynamic_slice_in_dim(dk_acc, block_start, key_span, 0) + grad_k, block_start, 0)
        dv_acc = lax.dynamic_update_slice_in_dim(dv_acc, lax.dynamic_slice_in_dim(dv_acc, block_start, key_span, 0) + grad_v, block_start, 0)
        return ((dk_acc, dv_acc), grad_q)
    start_pair = (jnp.zeros((WINDOW + length, key_width), jnp.float32), jnp.zeros((WINDOW + length, key_width), jnp.float32))
    (dk_acc, dv_acc), dq_blocks = lax.scan(advance, start_pair, jnp.arange(blocks, dtype=jnp.int32))
    dq_rot = dq_blocks.reshape(length, QH * HD)
    dk_rot = dk_acc[WINDOW:]
    grad_v = dv_acc[WINDOW:]
    grad_q_raw, grad_q_gain = q_back(dq_rot)
    grad_k_raw, grad_k_gain = k_back(dk_rot)
    return (grad_q_raw.astype(jnp.bfloat16), grad_k_raw.astype(jnp.bfloat16), grad_v.astype(jnp.bfloat16), grad_q_gain, grad_k_gain)

def reference(q_raw, k_raw, values, grad_out, q_gain, k_gain):

    def per_sequence(items):
        return one_sequence(items[0], items[1], items[2], items[3], q_gain, k_gain)
    grad_q, grad_k, grad_v, gains_q, gains_k = lax.map(per_sequence, (q_raw, k_raw, values, grad_out))
    return (grad_q, grad_k, grad_v, lax.optimization_barrier(jnp.sum(gains_q, axis=0)), lax.optimization_barrier(jnp.sum(gains_k, axis=0)))
```

```python
import jax
import jax.numpy as jnp
from jax import lax
from jax.experimental import pallas as pl
from jax.experimental.pallas import tpu as pltpu
from jax.sharding import PartitionSpec as P

WINDOW = 1024


EPS = 1e-06
ROPE_BASE = 10000.0
MASKED = -1e30


def from_behind(array, by):
    count = lax.axis_size("seq")
    pairs = [(i, i + by) for i in range(count) if 0 <= i + by < count]
    return lax.ppermute(array, "seq", pairs)


def core_swap(array):
    count = lax.axis_size("seq")
    return lax.ppermute(array, "seq", [(i, i ^ 1) for i in range(count)])


LOW = 8
X_SIZE = 4


def gain_sum_kernel(seq_size, dp_size, x_ref, o_ref, slots_a, slots_b, slots_c, part_b, part_c, send_sem, recv_sem):
    seq = lax.axis_index("seq")
    dp = lax.axis_index("dp")
    z_lo_size = seq_size // LOW
    z_size = z_lo_size * (dp_size // X_SIZE)
    low = lax.rem(seq, LOW)
    z_lo = lax.div(seq, LOW)
    x_pos = lax.rem(dp, X_SIZE)
    z_pos = lax.div(dp, X_SIZE) * z_lo_size + z_lo

    def peer_a(k):
        return {"seq": z_lo * LOW + lax.rem(low + k, LOW), "dp": dp}

    def peer_b(k):
        return {"seq": seq, "dp": dp - x_pos + lax.rem(x_pos + k, X_SIZE)}

    def peer_c(k):
        z_other = lax.rem(z_pos + k, z_size)
        return {
            "seq": lax.rem(z_other, z_lo_size) * LOW + low,
            "dp": lax.div(z_other, z_lo_size) * X_SIZE + x_pos,
        }

    stages = ((LOW, peer_a, low), (X_SIZE, peer_b, x_pos), (z_size, peer_c, z_pos))
    barrier = pltpu.get_barrier_semaphore()
    total = 0
    for size, peer, _ in reversed(stages):
        for k in range(1, size):
            pl.semaphore_signal(barrier, inc=1, device_id=peer(k), device_id_type=pl.DeviceIdType.MESH)
            total += 1
    pl.semaphore_wait(barrier, total)

    base = 0
    sources = (x_ref, part_b, part_c)
    results = (part_b, part_c, o_ref)
    for (size, peer, mine), source, slots, result in zip(
        stages, sources, (slots_a, slots_b, slots_c), results
    ):
        copies = []
        for k in range(1, size):
            copy = pltpu.make_async_remote_copy(
                src_ref=source,
                dst_ref=slots.at[k],
                send_sem=send_sem.at[base + k - 1],
                recv_sem=recv_sem.at[base + k - 1],
                device_id=peer(k),
                device_id_type=pl.DeviceIdType.MESH,
            )
            copy.start()
            copies.append(copy)
        slots[0] = source[...]
        for copy in copies:
            copy.wait()
        acc = slots[lax.rem(mine + size, size)]
        for j in range(1, size):
            acc = acc + slots[lax.rem(mine - j + size, size)]
        result[...] = acc
        base += size - 1


def gain_sum(gains):
    seq_size = lax.axis_size("seq")
    dp_size = lax.axis_size("dp")
    z_size = seq_size // LOW * (dp_size // X_SIZE)
    peers = LOW + X_SIZE + z_size - 3
    return pl.pallas_call(
        lambda *refs: gain_sum_kernel(seq_size, dp_size, *refs),
        out_shape=jax.ShapeDtypeStruct(gains.shape, jnp.float32),
        in_specs=[pl.BlockSpec(memory_space=pltpu.VMEM)],
        out_specs=pl.BlockSpec(memory_space=pltpu.VMEM),
        scratch_shapes=[
            pltpu.VMEM((LOW,) + gains.shape, jnp.float32),
            pltpu.VMEM((X_SIZE,) + gains.shape, jnp.float32),
            pltpu.VMEM((z_size,) + gains.shape, jnp.float32),
            pltpu.VMEM(gains.shape, jnp.float32),
            pltpu.VMEM(gains.shape, jnp.float32),
            pltpu.SemaphoreType.DMA((peers,)),
            pltpu.SemaphoreType.DMA((peers,)),
        ],
        compiler_params=pltpu.CompilerParams(collective_id=0, has_side_effects=True),
        name="gain_sum",
    )(gains)


def rope_tables(positions, head_size):
    half_size = head_size // 2
    freqs = jnp.power(ROPE_BASE, -(2.0 * jnp.arange(half_size, dtype=jnp.float32)) / head_size)
    angles = positions.astype(jnp.float32)[:, None] * freqs[None, :]
    return (jnp.cos(angles), jnp.sin(angles))


def norm_rope(raw_in, gain_in, cosine, sine, head_count):
    head_size = gain_in.shape[0]
    row_count = raw_in.shape[0]
    inputs = raw_in.reshape(row_count, head_count, head_size)
    inverse = lax.rsqrt(jnp.mean(inputs * inputs, axis=-1, keepdims=True) + EPS)
    scaled = inputs * inverse * gain_in
    half_size = head_size // 2
    lower = scaled[..., :half_size]
    upper = scaled[..., half_size:]
    cos_rows = cosine[:, None, :]
    sin_rows = sine[:, None, :]
    turned = jnp.concatenate(
        [lower * cos_rows - upper * sin_rows, upper * cos_rows + lower * sin_rows], axis=-1
    )
    return turned.reshape(row_count, head_count * head_size)


def local(q_raw, k_raw, values, grad_out, q_gain, k_gain):
    q_local = q_raw[0]
    k_local = k_raw[0]
    v_local = values[0]
    do_local = grad_out[0]
    rows_here = q_local.shape[0]
    head_size = q_gain.shape[0]
    query_heads = q_local.shape[1] // head_size
    pair_heads = k_local.shape[1] // head_size
    group_size = query_heads // pair_heads
    reach_dev = WINDOW // rows_here
    key_span = WINDOW + rows_here
    score_scale = head_size ** (-0.5)
    first_pos = lax.axis_index("seq") * rows_here
    positions = first_pos + jnp.arange(rows_here, dtype=jnp.int32)
    cosine, sine = rope_tables(positions, head_size)
    q_rot32, q_back = jax.vjp(
        lambda raw_in, gain_in: norm_rope(raw_in, gain_in, cosine, sine, query_heads),
        q_local.astype(jnp.float32),
        q_gain,
    )
    k_rot32, k_back = jax.vjp(
        lambda raw_in, gain_in: norm_rope(raw_in, gain_in, cosine, sine, pair_heads),
        k_local.astype(jnp.float32),
        k_gain,
    )
    q_rot = q_rot32.astype(jnp.bfloat16)
    k_rot = k_rot32.astype(jnp.bfloat16)
    first_core = lax.rem(lax.axis_index("seq"), 2) == 0

    def halo(own):
        two = from_behind(own, 2)
        four = from_behind(two, 2)
        one = core_swap(jnp.where(first_core, own, two))
        three = core_swap(jnp.where(first_core, two, four))
        return jnp.concatenate([four, three, two, one, own], axis=0)

    key_rows = halo(k_rot)
    value_rows = halo(v_local)
    q_heads = q_rot.reshape(rows_here, pair_heads, group_size, head_size)
    k_heads = key_rows.reshape(key_span, pair_heads, head_size)
    v_heads = value_rows.reshape(key_span, pair_heads, head_size)
    do_heads = do_local.reshape(rows_here, pair_heads, group_size, head_size)
    query_idx = jnp.arange(rows_here, dtype=jnp.int32)[:, None]
    key_idx = jnp.arange(key_span, dtype=jnp.int32)[None, :]
    distance = query_idx + WINDOW - key_idx
    visible = (distance >= 0) & (distance < WINDOW) & (key_idx >= WINDOW - first_pos)
    scores = (
        jnp.einsum("tkgd,skd->kgts", q_heads, k_heads, preferred_element_type=jnp.float32)
        * score_scale
    )
    scores = jnp.where(visible, scores, MASKED)
    row_top = jnp.max(scores, axis=-1, keepdims=True)
    row_total = jnp.log(jnp.sum(jnp.exp(scores - row_top), axis=-1, keepdims=True)) + row_top
    weights = jnp.exp(scores - row_total)
    weights_b = weights.astype(jnp.bfloat16)
    dweights = jnp.einsum("tkgd,skd->kgts", do_heads, v_heads, preferred_element_type=jnp.float32)
    row_delta = jnp.sum(weights * dweights, axis=-1, keepdims=True)
    dscores = (weights * (dweights - row_delta) * score_scale).astype(jnp.bfloat16)
    dq_rot = jnp.einsum(
        "kgts,skd->tkgd", dscores, k_heads, preferred_element_type=jnp.float32
    ).reshape(rows_here, query_heads * head_size)
    dk_all = jnp.einsum("kgts,tkgd->skd", dscores, q_heads, preferred_element_type=jnp.float32)
    dv_all = jnp.einsum("kgts,tkgd->skd", weights_b, do_heads, preferred_element_type=jnp.float32)

    def collect(terms):
        def block(offset):
            low_row = (reach_dev - offset) * rows_here
            return terms[low_row : low_row + rows_here]

        one = core_swap(block(1).astype(jnp.bfloat16)).astype(jnp.float32)
        three = core_swap(block(3).astype(jnp.bfloat16)).astype(jnp.float32)
        own = block(0) + jnp.where(first_core, one, 0.0)
        two = block(2) + jnp.where(first_core, three, one)
        four = block(4) + jnp.where(first_core, 0.0, three)
        from_four = from_behind(four.astype(jnp.bfloat16), -2).astype(jnp.float32)
        from_two = from_behind((two + from_four).astype(jnp.bfloat16), -2)
        return own + from_two.astype(jnp.float32)

    dk_own = collect(dk_all)
    dv_own = collect(dv_all)
    dk_rot = dk_own.reshape(rows_here, pair_heads * head_size)
    grad_q_local, gain_q_local = q_back(dq_rot)
    grad_k_local, gain_k_local = k_back(dk_rot)
    gains = jnp.concatenate([gain_q_local, gain_k_local]).reshape(4, 128)
    gains = gain_sum(jnp.pad(gains, ((0, 4), (0, 0))))[:4].reshape(2, head_size)
    gain_q_all, gain_k_all = gains[0], gains[1]
    grad_v_local = dv_own.reshape(rows_here, pair_heads * head_size).astype(jnp.bfloat16)
    return (
        grad_q_local.astype(jnp.bfloat16)[None],
        grad_k_local.astype(jnp.bfloat16)[None],
        grad_v_local[None],
        gain_q_all,
        gain_k_all,
    )


def solution(mesh):
    return jax.shard_map(
        local,
        mesh=mesh,
        in_specs=(
            P("dp", "seq", None),
            P("dp", "seq", None),
            P("dp", "seq", None),
            P("dp", "seq", None),
            P(),
            P(),
        ),
        out_specs=(P("dp", "seq", None), P("dp", "seq", None), P("dp", "seq", None), P(), P()),
        check_vma=False,
    )
```

```python
import jax
import jax.numpy as jnp
from jax import lax
from jax.experimental import pallas as pl
from jax.experimental.pallas import tpu as pltpu
from jax.sharding import PartitionSpec as P

WINDOW = 1024


EPS = 1e-06
ROPE_BASE = 10000.0
MASKED = -1e30
MESH = pl.DeviceIdType.MESH

LOW = 8
X_SIZE = 4


def rope_tables(positions, head_size):
    half_size = head_size // 2
    freqs = jnp.power(ROPE_BASE, -(2.0 * jnp.arange(half_size, dtype=jnp.float32)) / head_size)
    angles = positions.astype(jnp.float32)[:, None] * freqs[None, :]
    return (jnp.cos(angles), jnp.sin(angles))


def norm_rope(raw_ref, out_ref, gain_ref, cosine, sine):
    head_size = gain_ref.shape[1]
    half = head_size // 2
    for start in range(0, raw_ref.shape[1], head_size):
        x = raw_ref[:, start : start + head_size].astype(jnp.float32)
        scaled = x * lax.rsqrt(jnp.mean(x * x, axis=-1, keepdims=True) + EPS) * gain_ref[...]
        lower, upper = scaled[:, :half], scaled[:, half:]
        out_ref[:, start : start + half] = (lower * cosine - upper * sine).astype(out_ref.dtype)
        out_ref[:, start + half : start + head_size] = (upper * cosine + lower * sine).astype(
            out_ref.dtype
        )


def norm_rope_back(raw_ref, grad_ref, out_ref, gain_ref, cosine, sine):
    head_size = gain_ref.shape[1]
    half = head_size // 2
    gain_grad = jnp.zeros((1, head_size), jnp.float32)
    for start in range(0, raw_ref.shape[1], head_size):
        x = raw_ref[:, start : start + head_size].astype(jnp.float32)
        inverse = lax.rsqrt(jnp.mean(x * x, axis=-1, keepdims=True) + EPS)
        normed = x * inverse
        lower = grad_ref[:, start : start + half]
        upper = grad_ref[:, start + half : start + head_size]
        d_scaled = jnp.concatenate(
            [lower * cosine + upper * sine, upper * cosine - lower * sine], axis=-1
        )
        gain_grad = gain_grad + jnp.sum(d_scaled * normed, axis=0, keepdims=True)
        d_normed = d_scaled * gain_ref[...]
        along = jnp.mean(d_normed * normed, axis=-1, keepdims=True)
        out_ref[:, start : start + head_size] = (inverse * (d_normed - normed * along)).astype(
            out_ref.dtype
        )
    return gain_grad


def greet_neighbours(seq, count):
    barrier = pltpu.get_barrier_semaphore()
    pl.semaphore_signal(barrier, inc=1, device_id={"seq": other_core(seq)}, device_id_type=MESH)

    @pl.when(seq >= 2)
    def _():
        pl.semaphore_signal(barrier, inc=1, device_id={"seq": seq - 2}, device_id_type=MESH)

    @pl.when(seq + 2 < count)
    def _():
        pl.semaphore_signal(barrier, inc=1, device_id={"seq": seq + 2}, device_id_type=MESH)

    inside = (seq >= 2) & (seq + 2 < count)

    @pl.when(inside)
    def _():
        pl.semaphore_wait(barrier, 3)

    @pl.when(jnp.logical_not(inside))
    def _():
        pl.semaphore_wait(barrier, 2)


def other_core(seq):
    return seq + 1 - 2 * lax.rem(seq, 2)


def halo_kernel(
    count, q_ref, k_ref, v_ref, q_gain_ref, k_gain_ref, cos_ref, sin_ref,
    q_out, k_out, v_out, send_sem, recv_sem, copy_sem,
):
    seq = lax.axis_index("seq")
    core = lax.rem(seq, 2)
    cosine, sine = cos_ref[...], sin_ref[...]
    outs = (v_out, k_out)

    def send(which, source, target, hop, device):
        return pltpu.make_async_remote_copy(
            src_ref=outs[which].at[source],
            dst_ref=outs[which].at[target],
            send_sem=send_sem.at[which, hop],
            recv_sem=recv_sem.at[which, hop],
            device_id={"seq": device},
            device_id_type=MESH,
        )

    ahead = seq + 2
    beside = other_core(seq)
    local = pltpu.make_async_copy(v_ref, v_out.at[4], copy_sem)
    local.start()
    greet_neighbours(seq, count)
    local.wait()

    def send_own(which):
        @pl.when(ahead < count)
        def _():
            send(which, 4, 2, 0, ahead).start()

    send_own(0)
    norm_rope(k_ref, k_out.at[4], k_gain_ref, cosine, sine)
    send_own(1)
    for which in range(2):

        @pl.when(core == 0)
        def _():
            send(which, 4, 3, 2, beside).start()

        @pl.when(seq < 4)
        def _():
            outs[which][0] = jnp.zeros(outs[which].shape[1:], outs[which].dtype)

        @pl.when(seq < 3)
        def _():
            outs[which][1] = jnp.zeros(outs[which].shape[1:], outs[which].dtype)

        @pl.when(seq < 2)
        def _():
            outs[which][2] = jnp.zeros(outs[which].shape[1:], outs[which].dtype)

        @pl.when(seq < 1)
        def _():
            outs[which][3] = jnp.zeros(outs[which].shape[1:], outs[which].dtype)

    norm_rope(q_ref, q_out, q_gain_ref, cosine, sine)
    for which in range(2):

        @pl.when(seq >= 2)
        def _():
            send(which, 4, 2, 0, ahead).wait_recv()

            @pl.when(ahead < count)
            def _():
                send(which, 2, 0, 1, ahead).start()

            @pl.when(core == 0)
            def _():
                send(which, 2, 1, 3, beside).start()

            @pl.when(core == 1)
            def _():
                send(which, 2, 3, 2, beside).start()

    for which in range(2):

        @pl.when(seq >= 4)
        def _():
            send(which, 2, 0, 1, ahead).wait_recv()

            @pl.when(core == 1)
            def _():
                send(which, 0, 1, 3, beside).start()

    for which in range(2):

        @pl.when(seq >= 1)
        def _():
            send(which, 4, 3, 2, beside).wait_recv()

        @pl.when(seq >= 3)
        def _():
            send(which, 2, 1, 3, beside).wait_recv()

        @pl.when(ahead < count)
        def _():
            send(which, 4, 2, 0, ahead).wait_send()

            @pl.when(seq >= 2)
            def _():
                send(which, 2, 0, 1, ahead).wait_send()

        @pl.when((core == 0) | (seq >= 2))
        def _():
            send(which, 4, 3, 2, beside).wait_send()

        @pl.when(seq >= 2 + 2 * core)
        def _():
            send(which, 2, 1, 3, beside).wait_send()


def attention_kernel(
    q_ref, k_ref, v_ref, do_ref, dq_ref, gk_ref, gv_ref, gk_own_ref, gv_own_ref, ds_ref, w_ref
):
    rows, head_size = q_ref.shape
    span = k_ref.shape[0]
    scale = head_size ** (-0.5)
    head = lax.rem(pl.program_id(0), 2)
    first_pos = lax.axis_index("seq") * rows
    row = lax.broadcasted_iota(jnp.int32, (rows, span), 0)
    key = lax.broadcasted_iota(jnp.int32, (rows, span), 1)
    visible = (key > row) & (key <= row + WINDOW) & (key >= WINDOW - first_pos)
    across = (((1,), (1,)), ((), ()))
    scores = lax.dot_general(q_ref[...], k_ref[...], across, preferred_element_type=jnp.float32)
    scores = jnp.where(visible, scores * scale, MASKED)
    top = jnp.max(scores, axis=-1, keepdims=True)
    powers = jnp.exp(scores - top)
    weights = powers * (1.0 / jnp.sum(powers, axis=-1, keepdims=True))
    dweights = lax.dot_general(do_ref[...], v_ref[...], across, preferred_element_type=jnp.float32)
    delta = jnp.sum(weights * dweights, axis=-1, keepdims=True)
    dscores = (weights * (dweights - delta) * scale).astype(jnp.bfloat16)
    dq_ref[...] = jnp.dot(dscores, k_ref[...], preferred_element_type=jnp.float32)
    down = (((0,), (0,)), ((), ()))
    dk = lax.dot_general(dscores, q_ref[...], down, preferred_element_type=jnp.float32)
    dv = lax.dot_general(
        weights.astype(jnp.bfloat16), do_ref[...], down, preferred_element_type=jnp.float32
    )

    @pl.when(head == 0)
    def _():
        ds_ref[...] = dk
        w_ref[...] = dv

    @pl.when(head == 1)
    def _():
        dk_sum = ds_ref[...] + dk
        dv_sum = w_ref[...] + dv
        gk_ref[...] = dk_sum[:WINDOW].astype(jnp.bfloat16)
        gv_ref[...] = dv_sum[:WINDOW].astype(jnp.bfloat16)
        gk_own_ref[...] = dk_sum[WINDOW:]
        gv_own_ref[...] = dv_sum[WINDOW:]


def collect_kernel(
    count, gk_ref, gv_ref, gk_own_ref, gv_own_ref, q_ref, dq_ref, q_gain_ref, cos_ref, sin_ref,
    dk_out, dv_out, q_out, gain_out, beside_buf, behind_buf, sent_buf, send_sem, recv_sem,
):
    seq = lax.axis_index("seq")
    core = lax.rem(seq, 2)
    terms = (gk_ref, gv_ref)
    behind = seq - 2
    beside = other_core(seq)

    def swap(which, part):
        return pltpu.make_async_remote_copy(
            src_ref=terms[which].at[3 - 2 * part],
            dst_ref=beside_buf.at[which, part],
            send_sem=send_sem.at[which, part],
            recv_sem=recv_sem.at[which, part],
            device_id={"seq": beside},
            device_id_type=MESH,
        )

    def hop(which, part):
        return pltpu.make_async_remote_copy(
            src_ref=sent_buf.at[which, part],
            dst_ref=behind_buf.at[which, part],
            send_sem=send_sem.at[which, 2 + part],
            recv_sem=recv_sem.at[which, 2 + part],
            device_id={"seq": behind},
            device_id_type=MESH,
        )

    greet_neighbours(seq, count)
    for which in range(2):
        swap(which, 1).start()
        swap(which, 0).start()
    for which in range(2):
        swap(which, 1).wait()
        four = terms[which][0].astype(jnp.float32)

        @pl.when(core == 0)
        def _():
            sent_buf[which, 0] = terms[which][0]

        @pl.when(core == 1)
        def _():
            sent_buf[which, 0] = (four + beside_buf[which, 1].astype(jnp.float32)).astype(
                jnp.bfloat16
            )

        @pl.when(seq >= 2)
        def _():
            hop(which, 0).start()

    gain_grad = norm_rope_back(q_ref, dq_ref, q_out, q_gain_ref, cos_ref[...], sin_ref[...])
    half = gain_grad.shape[1] // 2
    gain_out[...] = jnp.zeros_like(gain_out)
    gain_out[0:1, :] = gain_grad[:, :half]
    gain_out[1:2, :] = gain_grad[:, half:]
    for which in range(2):
        swap(which, 0).wait()
        two = terms[which][2].astype(jnp.float32) + beside_buf[which, 1 - core].astype(jnp.float32)

        @pl.when(seq + 2 < count)
        def _():
            hop(which, 0).wait_recv()
            sent_buf[which, 1] = (two + behind_buf[which, 0].astype(jnp.float32)).astype(
                jnp.bfloat16
            )

        @pl.when(seq + 2 >= count)
        def _():
            sent_buf[which, 1] = two.astype(jnp.bfloat16)

        @pl.when(seq >= 2)
        def _():
            hop(which, 1).start()

    for which, (own_ref, out) in enumerate(((gk_own_ref, dk_out), (gv_own_ref, dv_out))):

        @pl.when(seq + 2 < count)
        def _():
            hop(which, 1).wait_recv()

        @pl.when(seq + 2 >= count)
        def _():
            behind_buf[which, 1] = jnp.zeros(behind_buf.shape[2:], behind_buf.dtype)

        total = own_ref[...] + behind_buf[which, 1].astype(jnp.float32)

        @pl.when(core == 0)
        def _():
            out[...] = (total + beside_buf[which, 0].astype(jnp.float32)).astype(out.dtype)

        @pl.when(core == 1)
        def _():
            out[...] = total.astype(out.dtype)

    for which in range(2):

        @pl.when(seq >= 2)
        def _():
            hop(which, 0).wait_send()
            hop(which, 1).wait_send()


def gain_sum_kernel(
    seq_size, dp_size, k_ref, dk_ref, gain_ref, k_gain_ref, cos_ref, sin_ref, k_out, o_ref,
    x_ref, slots_a, slots_b, slots_c, part_b, part_c, send_sem, recv_sem,
):
    seq = lax.axis_index("seq")
    dp = lax.axis_index("dp")
    z_lo_size = seq_size // LOW
    z_size = z_lo_size * (dp_size // X_SIZE)
    low = lax.rem(seq, LOW)
    z_lo = lax.div(seq, LOW)
    x_pos = lax.rem(dp, X_SIZE)
    z_pos = lax.div(dp, X_SIZE) * z_lo_size + z_lo

    def peer_a(k):
        return {"seq": z_lo * LOW + lax.rem(low + k, LOW), "dp": dp}

    def peer_b(k):
        return {"seq": seq, "dp": dp - x_pos + lax.rem(x_pos + k, X_SIZE)}

    def peer_c(k):
        z_other = lax.rem(z_pos + k, z_size)
        return {
            "seq": lax.rem(z_other, z_lo_size) * LOW + low,
            "dp": lax.div(z_other, z_lo_size) * X_SIZE + x_pos,
        }

    stages = ((LOW, peer_a, low), (X_SIZE, peer_b, x_pos), (z_size, peer_c, z_pos))
    barrier = pltpu.get_barrier_semaphore()
    total = 0
    for size, peer, _ in reversed(stages):
        for k in range(1, size):
            pl.semaphore_signal(barrier, inc=1, device_id=peer(k), device_id_type=MESH)
            total += 1
    gain_grad = norm_rope_back(k_ref, dk_ref, k_out, k_gain_ref, cos_ref[...], sin_ref[...])
    half = gain_grad.shape[1] // 2
    x_ref[...] = gain_ref[...]
    x_ref[2:3, :] = gain_grad[:, :half]
    x_ref[3:4, :] = gain_grad[:, half:]
    pl.semaphore_wait(barrier, total)

    base = 0
    sources = (x_ref, part_b, part_c)
    results = (part_b, part_c, o_ref)
    for (size, peer, mine), source, slots, result in zip(
        stages, sources, (slots_a, slots_b, slots_c), results
    ):
        copies = []
        for k in range(1, size):
            copy = pltpu.make_async_remote_copy(
                src_ref=source,
                dst_ref=slots.at[k],
                send_sem=send_sem.at[base + k - 1],
                recv_sem=recv_sem.at[base + k - 1],
                device_id=peer(k),
                device_id_type=MESH,
            )
            copy.start()
            copies.append(copy)
        slots[0] = source[...]
        for copy in copies:
            copy.wait()
        acc = slots[lax.rem(mine + size, size)]
        for j in range(1, size):
            acc = acc + slots[lax.rem(mine - j + size, size)]
        result[...] = acc
        base += size - 1


VMEM_SPEC = pl.BlockSpec(memory_space=pltpu.VMEM)


def halo(seq_size, *args):
    q, k = args[0], args[1]
    return pl.pallas_call(
        lambda *refs: halo_kernel(seq_size, *refs),
        out_shape=(
            jax.ShapeDtypeStruct(q.shape, jnp.bfloat16),
            jax.ShapeDtypeStruct((5,) + k.shape, jnp.bfloat16),
            jax.ShapeDtypeStruct((5,) + k.shape, jnp.bfloat16),
        ),
        in_specs=[VMEM_SPEC] * 7,
        out_specs=(VMEM_SPEC,) * 3,
        scratch_shapes=[
            pltpu.SemaphoreType.DMA((2, 4)),
            pltpu.SemaphoreType.DMA((2, 4)),
            pltpu.SemaphoreType.DMA,
        ],
        compiler_params=pltpu.CompilerParams(collective_id=1, has_side_effects=True),
        name="halo",
    )(*args)


def attention(q, keys, vals, grad_out, head_size):
    rows = q.shape[0]
    span = keys.shape[0]
    heads = q.shape[1] // head_size

    def by_head(height):
        return pl.BlockSpec((height, head_size), lambda h: (0, h))

    def by_group(height):
        return pl.BlockSpec((height, head_size), lambda h: (0, h // 2))

    def group_shape(height, dtype):
        return jax.ShapeDtypeStruct((height, keys.shape[1]), dtype)

    return pl.pallas_call(
        attention_kernel,
        grid=(heads,),
        out_shape=(
            jax.ShapeDtypeStruct(q.shape, jnp.float32),
            group_shape(WINDOW, jnp.bfloat16),
            group_shape(WINDOW, jnp.bfloat16),
            group_shape(rows, jnp.float32),
            group_shape(rows, jnp.float32),
        ),
        in_specs=[by_head(rows), by_group(span), by_group(span), by_head(rows)],
        out_specs=(by_head(rows), by_group(WINDOW), by_group(WINDOW), by_group(rows), by_group(rows)),
        scratch_shapes=[
            pltpu.VMEM((span, head_size), jnp.float32),
            pltpu.VMEM((span, head_size), jnp.float32),
        ],
        name="attention",
    )(q, keys, vals, grad_out)


def collect(seq_size, *args):
    own, q = args[2], args[4]
    rows, columns = own.shape
    return pl.pallas_call(
        lambda *refs: collect_kernel(seq_size, *refs),
        out_shape=(
            jax.ShapeDtypeStruct(own.shape, jnp.float32),
            jax.ShapeDtypeStruct(own.shape, jnp.bfloat16),
            jax.ShapeDtypeStruct(q.shape, jnp.bfloat16),
            jax.ShapeDtypeStruct((8, 128), jnp.float32),
        ),
        in_specs=[VMEM_SPEC] * 9,
        out_specs=(VMEM_SPEC,) * 4,
        scratch_shapes=[
            pltpu.VMEM((2, 2, rows, columns), jnp.bfloat16),
            pltpu.VMEM((2, 2, rows, columns), jnp.bfloat16),
            pltpu.VMEM((2, 2, rows, columns), jnp.bfloat16),
            pltpu.SemaphoreType.DMA((2, 4)),
            pltpu.SemaphoreType.DMA((2, 4)),
        ],
        compiler_params=pltpu.CompilerParams(collective_id=2, has_side_effects=True),
        name="collect",
    )(*args)


def gain_sum(seq_size, dp_size, *args):
    k, gains = args[0], args[2]
    z_size = seq_size // LOW * (dp_size // X_SIZE)
    peers = LOW + X_SIZE + z_size - 3
    return pl.pallas_call(
        lambda *refs: gain_sum_kernel(seq_size, dp_size, *refs),
        out_shape=(
            jax.ShapeDtypeStruct(k.shape, jnp.bfloat16),
            jax.ShapeDtypeStruct(gains.shape, jnp.float32),
        ),
        in_specs=[VMEM_SPEC] * 6,
        out_specs=(VMEM_SPEC,) * 2,
        scratch_shapes=[
            pltpu.VMEM(gains.shape, jnp.float32),
            pltpu.VMEM((LOW,) + gains.shape, jnp.float32),
            pltpu.VMEM((X_SIZE,) + gains.shape, jnp.float32),
            pltpu.VMEM((z_size,) + gains.shape, jnp.float32),
            pltpu.VMEM(gains.shape, jnp.float32),
            pltpu.VMEM(gains.shape, jnp.float32),
            pltpu.SemaphoreType.DMA((peers,)),
            pltpu.SemaphoreType.DMA((peers,)),
        ],
        compiler_params=pltpu.CompilerParams(collective_id=0, has_side_effects=True),
        name="gain_sum",
    )(*args)


def local(seq_size, dp_size, q_raw, k_raw, values, grad_out, q_gain, k_gain):
    q_local, k_local, v_local, do_local = q_raw[0], k_raw[0], values[0], grad_out[0]
    rows, columns = k_local.shape
    head_size = q_gain.shape[0]
    positions = lax.axis_index("seq") * rows + jnp.arange(rows, dtype=jnp.int32)
    cosine, sine = rope_tables(positions, head_size)
    q_gain, k_gain = q_gain[None], k_gain[None]
    q_rot, keys, vals = halo(seq_size, q_local, k_local, v_local, q_gain, k_gain, cosine, sine)
    dq_rot, gk, gv, gk_own, gv_own = attention(
        q_rot, keys.reshape(5 * rows, columns), vals.reshape(5 * rows, columns), do_local, head_size
    )
    dk_rot, grad_v, grad_q, gains = collect(
        seq_size, gk.reshape(4, rows, columns), gv.reshape(4, rows, columns), gk_own, gv_own,
        q_local, dq_rot, q_gain, cosine, sine,
    )
    grad_k, gains = gain_sum(seq_size, dp_size, k_local, dk_rot, gains, k_gain, cosine, sine)
    gains = gains[:4].reshape(2, head_size)
    return (grad_q[None], grad_k[None], grad_v[None], gains[0], gains[1])


def solution(mesh):
    return jax.shard_map(
        lambda *args: local(mesh.shape["seq"], mesh.shape["dp"], *args),
        mesh=mesh,
        in_specs=(
            P("dp", "seq", None),
            P("dp", "seq", None),
            P("dp", "seq", None),
            P("dp", "seq", None),
            P(),
            P(),
        ),
        out_specs=(P("dp", "seq", None), P("dp", "seq", None), P("dp", "seq", None), P(), P()),
        check_vma=False,
    )
```

```python
import jax
import jax.numpy as jnp
from jax import lax
from jax.experimental import pallas as pl
from jax.experimental.pallas import tpu as pltpu
from jax.sharding import PartitionSpec as P

WINDOW = 1024


EPS = 1e-06
ROPE_BASE = 10000.0
MASKED = -1e30
MESH = pl.DeviceIdType.MESH

LOW = 8
X_SIZE = 4


def rope_tables(positions, head_size):
    half_size = head_size // 2
    freqs = jnp.power(ROPE_BASE, -(2.0 * jnp.arange(half_size, dtype=jnp.float32)) / head_size)
    angles = positions.astype(jnp.float32)[:, None] * freqs[None, :]
    return (jnp.cos(angles), jnp.sin(angles))


def norm_rope(raw_ref, out_ref, gain_ref, cosine, sine):
    head_size = gain_ref.shape[1]
    half = head_size // 2
    for start in range(0, raw_ref.shape[1], head_size):
        x = raw_ref[:, start : start + head_size].astype(jnp.float32)
        scaled = x * lax.rsqrt(jnp.mean(x * x, axis=-1, keepdims=True) + EPS) * gain_ref[...]
        lower, upper = scaled[:, :half], scaled[:, half:]
        out_ref[:, start : start + half] = (lower * cosine - upper * sine).astype(out_ref.dtype)
        out_ref[:, start + half : start + head_size] = (upper * cosine + lower * sine).astype(
            out_ref.dtype
        )


def norm_rope_back(raw_ref, grad_ref, out_ref, gain_ref, cosine, sine):
    head_size = gain_ref.shape[1]
    half = head_size // 2
    gain_grad = jnp.zeros((1, head_size), jnp.float32)
    for start in range(0, raw_ref.shape[1], head_size):
        x = raw_ref[:, start : start + head_size].astype(jnp.float32)
        inverse = lax.rsqrt(jnp.mean(x * x, axis=-1, keepdims=True) + EPS)
        normed = x * inverse
        lower = grad_ref[:, start : start + half]
        upper = grad_ref[:, start + half : start + head_size]
        d_scaled = jnp.concatenate(
            [lower * cosine + upper * sine, upper * cosine - lower * sine], axis=-1
        )
        gain_grad = gain_grad + jnp.sum(d_scaled * normed, axis=0, keepdims=True)
        d_normed = d_scaled * gain_ref[...]
        along = jnp.mean(d_normed * normed, axis=-1, keepdims=True)
        out_ref[:, start : start + head_size] = (inverse * (d_normed - normed * along)).astype(
            out_ref.dtype
        )
    return gain_grad


def greet_signals(barrier, seq, count):
    pl.semaphore_signal(barrier, inc=1, device_id={"seq": other_core(seq)}, device_id_type=MESH)

    @pl.when(seq >= 2)
    def _():
        pl.semaphore_signal(barrier, inc=1, device_id={"seq": seq - 2}, device_id_type=MESH)

    @pl.when(seq + 2 < count)
    def _():
        pl.semaphore_signal(barrier, inc=1, device_id={"seq": seq + 2}, device_id_type=MESH)


def greet_waits(barrier, seq, count, others):
    inside = (seq >= 2) & (seq + 2 < count)

    @pl.when(inside)
    def _():
        pl.semaphore_wait(barrier, others + 3)

    @pl.when(jnp.logical_not(inside))
    def _():
        pl.semaphore_wait(barrier, others + 2)


def other_core(seq):
    return seq + 1 - 2 * lax.rem(seq, 2)


def halo_kernel(
    count, q_ref, k_ref, v_ref, q_gain_ref, k_gain_ref, cos_ref, sin_ref,
    q_out, k_out, v_out, send_sem, recv_sem, copy_sem,
):
    seq = lax.axis_index("seq")
    core = lax.rem(seq, 2)
    cosine, sine = cos_ref[...], sin_ref[...]
    outs = (v_out, k_out)

    def send(which, source, target, hop, device):
        return pltpu.make_async_remote_copy(
            src_ref=outs[which].at[source],
            dst_ref=outs[which].at[target],
            send_sem=send_sem.at[which, hop],
            recv_sem=recv_sem.at[which, hop],
            device_id={"seq": device},
            device_id_type=MESH,
        )

    ahead = seq + 2
    beside = other_core(seq)
    local = pltpu.make_async_copy(v_ref, v_out.at[4], copy_sem)
    local.start()
    barrier = pltpu.get_barrier_semaphore()
    greet_signals(barrier, seq, count)
    greet_waits(barrier, seq, count, 0)
    local.wait()

    def send_own(which):
        @pl.when(ahead < count)
        def _():
            send(which, 4, 2, 0, ahead).start()

    send_own(0)
    norm_rope(k_ref, k_out.at[4], k_gain_ref, cosine, sine)
    send_own(1)
    for which in range(2):

        @pl.when(core == 0)
        def _():
            send(which, 4, 3, 2, beside).start()

        @pl.when(seq < 4)
        def _():
            outs[which][0] = jnp.zeros(outs[which].shape[1:], outs[which].dtype)

        @pl.when(seq < 3)
        def _():
            outs[which][1] = jnp.zeros(outs[which].shape[1:], outs[which].dtype)

        @pl.when(seq < 2)
        def _():
            outs[which][2] = jnp.zeros(outs[which].shape[1:], outs[which].dtype)

        @pl.when(seq < 1)
        def _():
            outs[which][3] = jnp.zeros(outs[which].shape[1:], outs[which].dtype)

    norm_rope(q_ref, q_out, q_gain_ref, cosine, sine)
    for which in range(2):

        @pl.when(seq >= 2)
        def _():
            send(which, 4, 2, 0, ahead).wait_recv()

            @pl.when(ahead < count)
            def _():
                send(which, 2, 0, 1, ahead).start()

            @pl.when(core == 0)
            def _():
                send(which, 2, 1, 3, beside).start()

            @pl.when(core == 1)
            def _():
                send(which, 2, 3, 2, beside).start()

    for which in range(2):

        @pl.when(seq >= 4)
        def _():
            send(which, 2, 0, 1, ahead).wait_recv()

            @pl.when(core == 1)
            def _():
                send(which, 0, 1, 3, beside).start()

    for which in range(2):

        @pl.when(seq >= 1)
        def _():
            send(which, 4, 3, 2, beside).wait_recv()

        @pl.when(seq >= 3)
        def _():
            send(which, 2, 1, 3, beside).wait_recv()

        @pl.when(ahead < count)
        def _():
            send(which, 4, 2, 0, ahead).wait_send()

            @pl.when(seq >= 2)
            def _():
                send(which, 2, 0, 1, ahead).wait_send()

        @pl.when((core == 0) | (seq >= 2))
        def _():
            send(which, 4, 3, 2, beside).wait_send()

        @pl.when(seq >= 2 + 2 * core)
        def _():
            send(which, 2, 1, 3, beside).wait_send()


def attention_group(group, q_ref, keys_ref, vals_ref, do_ref, dq_ref, terms, owns):
    count, rows, columns = keys_ref.shape
    head_size = columns // 2
    span = count * rows
    scale = head_size ** (-0.5)
    lanes = slice(group * head_size, (group + 1) * head_size)
    first_pos = lax.axis_index("seq") * rows
    row = lax.broadcasted_iota(jnp.int32, (rows, span), 0)
    key = lax.broadcasted_iota(jnp.int32, (rows, span), 1)
    visible = (key > row) & (key <= row + WINDOW) & (key >= WINDOW - first_pos)
    across = (((1,), (1,)), ((), ()))
    down = (((0,), (0,)), ((), ()))
    keys = keys_ref[:, :, lanes].reshape(span, head_size)
    vals = vals_ref[:, :, lanes].reshape(span, head_size)
    sums = None
    for head in (2 * group, 2 * group + 1):
        cols = slice(head * head_size, (head + 1) * head_size)
        q, do = q_ref[:, cols], do_ref[:, cols]
        scores = lax.dot_general(q, keys, across, preferred_element_type=jnp.float32)
        scores = jnp.where(visible, scores * scale, MASKED)
        top = jnp.max(scores, axis=-1, keepdims=True)
        powers = jnp.exp(scores - top)
        weights = powers * (1.0 / jnp.sum(powers, axis=-1, keepdims=True))
        dweights = lax.dot_general(do, vals, across, preferred_element_type=jnp.float32)
        delta = jnp.sum(weights * dweights, axis=-1, keepdims=True)
        dscores = (weights * (dweights - delta) * scale).astype(jnp.bfloat16)
        dq_ref[:, cols] = jnp.dot(dscores, keys, preferred_element_type=jnp.float32)
        grads = (
            lax.dot_general(dscores, q, down, preferred_element_type=jnp.float32),
            lax.dot_general(
                weights.astype(jnp.bfloat16), do, down, preferred_element_type=jnp.float32
            ),
        )
        sums = grads if sums is None else tuple(x + y for x, y in zip(sums, grads))
    for which in range(2):
        behind = sums[which][:WINDOW].reshape(count - 1, rows, head_size)
        terms[which, :, :, lanes] = behind.astype(jnp.bfloat16)
        owns[which, :, lanes] = sums[which][WINDOW:]


def key_gain_grad(keys_ref, terms, owns, cosine, sine, turn_ref, gain_ref):
    count, rows, columns = keys_ref.shape
    head_size = columns // 2
    half = head_size // 2
    twice_cos = cosine * cosine - sine * sine
    twice_sin = 2.0 * cosine * sine
    same = jnp.zeros((1, half), jnp.float32)
    turned = jnp.zeros((1, half), jnp.float32)
    for block in range(count):
        real = jnp.zeros((1, half), jnp.float32)
        imag = jnp.zeros((1, half), jnp.float32)
        for start in (0, head_size):
            lower, upper = slice(start, start + half), slice(start + half, start + head_size)
            if block < count - 1:
                a_low = terms[0, block, :, lower].astype(jnp.float32)
                a_up = terms[0, block, :, upper].astype(jnp.float32)
            else:
                a_low, a_up = owns[0, :, lower], owns[0, :, upper]
            b_low = keys_ref[block, :, lower].astype(jnp.float32)
            b_up = keys_ref[block, :, upper].astype(jnp.float32)
            low, up = a_low * b_low, a_up * b_up
            x, y = low - up, a_low * b_up + a_up * b_low
            same = same + jnp.sum(low + up, axis=0, keepdims=True)
            real = real + jnp.sum(x * twice_cos + y * twice_sin, axis=0, keepdims=True)
            imag = imag + jnp.sum(y * twice_cos - x * twice_sin, axis=0, keepdims=True)
        turned = (
            turned
            + real * turn_ref[block : block + 1, :half]
            - imag * turn_ref[block : block + 1, half:]
        )
    grad = jnp.concatenate([same + turned, same - turned], axis=-1) * 0.5
    return grad / gain_ref[...]


def backward_kernel(
    seq_size, dp_size, q_rot_ref, keys_ref, vals_ref, do_ref, q_ref, k_ref, q_gain_ref, k_gain_ref,
    cos_ref, sin_ref, turn_ref, q_out, k_out, v_out, q_gain_out, k_gain_out,
    dq_ref, terms, owns, beside_buf, behind_buf, sent_buf, send_sem, recv_sem,
    x_ref, slots_a, slots_b, slots_c, part_b, part_c, gain_send_sem, gain_recv_sem,
):
    seq = lax.axis_index("seq")
    dp = lax.axis_index("dp")
    core = lax.rem(seq, 2)
    behind = seq - 2
    beside = other_core(seq)
    cosine, sine = cos_ref[...], sin_ref[...]

    z_lo_size = seq_size // LOW
    z_size = z_lo_size * (dp_size // X_SIZE)
    low = lax.rem(seq, LOW)
    z_lo = lax.div(seq, LOW)
    x_pos = lax.rem(dp, X_SIZE)
    z_pos = lax.div(dp, X_SIZE) * z_lo_size + z_lo

    def peer_a(k):
        return {"seq": z_lo * LOW + lax.rem(low + k, LOW), "dp": dp}

    def peer_b(k):
        return {"seq": seq, "dp": dp - x_pos + lax.rem(x_pos + k, X_SIZE)}

    def peer_c(k):
        z_other = lax.rem(z_pos + k, z_size)
        return {
            "seq": lax.rem(z_other, z_lo_size) * LOW + low,
            "dp": lax.div(z_other, z_lo_size) * X_SIZE + x_pos,
        }

    stages = ((LOW, peer_a, low), (X_SIZE, peer_b, x_pos), (z_size, peer_c, z_pos))
    barrier = pltpu.get_barrier_semaphore()
    greeted = 0
    for size, peer, _ in reversed(stages):
        for k in range(1, size):
            pl.semaphore_signal(barrier, inc=1, device_id=peer(k), device_id_type=MESH)
            greeted += 1
    greet_signals(barrier, seq, seq_size)
    heads = (q_rot_ref, keys_ref, vals_ref, do_ref, dq_ref, terms, owns)
    attention_group(0, *heads)
    attention_group(1, *heads)
    greet_waits(barrier, seq, seq_size, greeted)

    def swap(which, part):
        return pltpu.make_async_remote_copy(
            src_ref=terms.at[which, 3 - 2 * part],
            dst_ref=beside_buf.at[which, part],
            send_sem=send_sem.at[which, part],
            recv_sem=recv_sem.at[which, part],
            device_id={"seq": beside},
            device_id_type=MESH,
        )

    def hop(which, part):
        return pltpu.make_async_remote_copy(
            src_ref=sent_buf.at[which, part],
            dst_ref=behind_buf.at[which, part],
            send_sem=send_sem.at[which, 2 + part],
            recv_sem=recv_sem.at[which, 2 + part],
            device_id={"seq": behind},
            device_id_type=MESH,
        )

    sources = (x_ref, part_b, part_c)
    results = (part_b, part_c, x_ref)
    slot_refs = (slots_a, slots_b, slots_c)
    bases = (0, LOW - 1, LOW + X_SIZE - 2)

    def gain_copies(stage):
        size, peer, _ = stages[stage]
        return [
            pltpu.make_async_remote_copy(
                src_ref=sources[stage],
                dst_ref=slot_refs[stage].at[k],
                send_sem=gain_send_sem.at[bases[stage] + k - 1],
                recv_sem=gain_recv_sem.at[bases[stage] + k - 1],
                device_id=peer(k),
                device_id_type=MESH,
            )
            for k in range(1, size)
        ]

    def gain_start(stage):
        for copy in gain_copies(stage):
            copy.start()
        slot_refs[stage][0] = sources[stage][...]

    def gain_end(stage):
        for copy in gain_copies(stage):
            copy.wait()
        size, _, mine = stages[stage]
        slots = slot_refs[stage]
        acc = slots[lax.rem(mine + size, size)]
        for j in range(1, size):
            acc = acc + slots[lax.rem(mine - j + size, size)]
        results[stage][...] = acc

    for which in range(2):
        swap(which, 1).start()
    for which in range(2):
        swap(which, 0).start()
    for which in range(2):
        swap(which, 1).wait()
        four = terms[which, 0]

        @pl.when(core == 0)
        def _():
            sent_buf[which, 0] = four

        @pl.when(core == 1)
        def _():
            sent_buf[which, 0] = (
                four.astype(jnp.float32) + beside_buf[which, 1].astype(jnp.float32)
            ).astype(jnp.bfloat16)

        @pl.when(seq >= 2)
        def _():
            hop(which, 0).start()

    k_gain = key_gain_grad(keys_ref, terms, owns, cosine, sine, turn_ref, k_gain_ref)
    q_gain = norm_rope_back(q_ref, dq_ref, q_out, q_gain_ref, cosine, sine)
    half = q_gain.shape[1] // 2
    x_ref[...] = jnp.zeros_like(x_ref)
    x_ref[0:1, :] = q_gain[:, :half]
    x_ref[1:2, :] = q_gain[:, half:]
    x_ref[2:3, :] = k_gain[:, :half]
    x_ref[3:4, :] = k_gain[:, half:]
    gain_start(0)
    for which in range(2):
        swap(which, 0).wait()
        two = terms[which, 2].astype(jnp.float32) + beside_buf[which, 1 - core].astype(jnp.float32)

        @pl.when(seq + 2 < seq_size)
        def _():
            hop(which, 0).wait_recv()
            sent_buf[which, 1] = (two + behind_buf[which, 0].astype(jnp.float32)).astype(
                jnp.bfloat16
            )

        @pl.when(seq + 2 >= seq_size)
        def _():
            sent_buf[which, 1] = two.astype(jnp.bfloat16)

        @pl.when(seq >= 2)
        def _():
            hop(which, 1).start()

        gain_end(which)
        gain_start(which + 1)

    for which in range(2):

        @pl.when(seq + 2 < seq_size)
        def _():
            hop(which, 1).wait_recv()
            owns[which] = owns[which] + behind_buf[which, 1].astype(jnp.float32)

        @pl.when(core == 0)
        def _():
            owns[which] = owns[which] + beside_buf[which, 0].astype(jnp.float32)

        if which == 0:
            norm_rope_back(k_ref, owns.at[0], k_out, k_gain_ref, cosine, sine)

    v_out[...] = owns[1].astype(v_out.dtype)
    gain_end(2)
    for out, start in ((q_gain_out, 0), (k_gain_out, 2)):
        out[:, :half] = x_ref[start : start + 1, :]
        out[:, half:] = x_ref[start + 1 : start + 2, :]
    for which in range(2):

        @pl.when(seq >= 2)
        def _():
            hop(which, 0).wait_send()
            hop(which, 1).wait_send()


VMEM_SPEC = pl.BlockSpec(memory_space=pltpu.VMEM)


def halo(seq_size, *args):
    q, k = args[0], args[1]
    return pl.pallas_call(
        lambda *refs: halo_kernel(seq_size, *refs),
        out_shape=(
            jax.ShapeDtypeStruct(q.shape, jnp.bfloat16),
            jax.ShapeDtypeStruct((5,) + k.shape, jnp.bfloat16),
            jax.ShapeDtypeStruct((5,) + k.shape, jnp.bfloat16),
        ),
        in_specs=[VMEM_SPEC] * 7,
        out_specs=(VMEM_SPEC,) * 3,
        scratch_shapes=[
            pltpu.SemaphoreType.DMA((2, 4)),
            pltpu.SemaphoreType.DMA((2, 4)),
            pltpu.SemaphoreType.DMA,
        ],
        compiler_params=pltpu.CompilerParams(collective_id=1, has_side_effects=True),
        name="halo",
    )(*args)


def backward(seq_size, dp_size, *args):
    q, keys, k = args[0], args[1], args[5]
    rows, columns = k.shape
    head_size = columns // 2
    z_size = seq_size // LOW * (dp_size // X_SIZE)
    peers = LOW + X_SIZE + z_size - 3
    gains = (8, 128)
    return pl.pallas_call(
        lambda *refs: backward_kernel(seq_size, dp_size, *refs),
        out_shape=(
            jax.ShapeDtypeStruct(q.shape, jnp.bfloat16),
            jax.ShapeDtypeStruct(k.shape, jnp.bfloat16),
            jax.ShapeDtypeStruct(k.shape, jnp.bfloat16),
            jax.ShapeDtypeStruct((1, head_size), jnp.float32),
            jax.ShapeDtypeStruct((1, head_size), jnp.float32),
        ),
        in_specs=[VMEM_SPEC] * 11,
        out_specs=(VMEM_SPEC,) * 5,
        scratch_shapes=[
            pltpu.VMEM(q.shape, jnp.float32),
            pltpu.VMEM((2, keys.shape[0] - 1, rows, columns), jnp.bfloat16),
            pltpu.VMEM((2, rows, columns), jnp.float32),
            pltpu.VMEM((2, 2, rows, columns), jnp.bfloat16),
            pltpu.VMEM((2, 2, rows, columns), jnp.bfloat16),
            pltpu.VMEM((2, 2, rows, columns), jnp.bfloat16),
            pltpu.SemaphoreType.DMA((2, 4)),
            pltpu.SemaphoreType.DMA((2, 4)),
            pltpu.VMEM(gains, jnp.float32),
            pltpu.VMEM((LOW,) + gains, jnp.float32),
            pltpu.VMEM((X_SIZE,) + gains, jnp.float32),
            pltpu.VMEM((z_size,) + gains, jnp.float32),
            pltpu.VMEM(gains, jnp.float32),
            pltpu.VMEM(gains, jnp.float32),
            pltpu.SemaphoreType.DMA((peers,)),
            pltpu.SemaphoreType.DMA((peers,)),
        ],
        compiler_params=pltpu.CompilerParams(collective_id=0, has_side_effects=True),
        name="backward",
    )(*args)


def local(seq_size, dp_size, q_raw, k_raw, values, grad_out, q_gain, k_gain):
    q_local, k_local, v_local, do_local = q_raw[0], k_raw[0], values[0], grad_out[0]
    rows = k_local.shape[0]
    head_size = q_gain.shape[0]
    positions = lax.axis_index("seq") * rows + jnp.arange(rows, dtype=jnp.int32)
    cosine, sine = rope_tables(positions, head_size)
    back = jnp.maximum(4 - jnp.arange(8, dtype=jnp.int32), 0) * (2 * rows)
    turn = jnp.concatenate(rope_tables(back, head_size), axis=-1)
    q_gain, k_gain = q_gain[None], k_gain[None]
    q_rot, keys, vals = halo(seq_size, q_local, k_local, v_local, q_gain, k_gain, cosine, sine)
    grad_q, grad_k, grad_v, grad_q_gain, grad_k_gain = backward(
        seq_size, dp_size, q_rot, keys, vals, do_local, q_local, k_local, q_gain, k_gain,
        cosine, sine, turn,
    )
    return (grad_q[None], grad_k[None], grad_v[None], grad_q_gain[0], grad_k_gain[0])


def solution(mesh):
    return jax.shard_map(
        lambda *args: local(mesh.shape["seq"], mesh.shape["dp"], *args),
        mesh=mesh,
        in_specs=(
            P("dp", "seq", None),
            P("dp", "seq", None),
            P("dp", "seq", None),
            P("dp", "seq", None),
            P(),
            P(),
        ),
        out_specs=(P("dp", "seq", None), P("dp", "seq", None), P("dp", "seq", None), P(), P()),
        check_vma=False,
    )
```

```python
import jax
import jax.numpy as jnp
import numpy as np
from jax import lax
from jax.experimental import pallas as pl
from jax.experimental.pallas import tpu as pltpu
from jax.sharding import PartitionSpec as P

WINDOW = 1024


EPS = 1e-06
ROPE_BASE = 10000.0
MASKED = -1e30
MESH = pl.DeviceIdType.MESH

LOW = 8
X_SIZE = 4


def rope_tables(positions, head_size):
    half_size = head_size // 2
    freqs = jnp.power(ROPE_BASE, -(2.0 * jnp.arange(half_size, dtype=jnp.float32)) / head_size)
    angles = positions.astype(jnp.float32)[:, None] * freqs[None, :]
    return (jnp.cos(angles), jnp.sin(angles))


def norm_rope(raw_ref, out_ref, gain_ref, cosine, sine):
    head_size = gain_ref.shape[1]
    half = head_size // 2
    for start in range(0, raw_ref.shape[1], head_size):
        x = raw_ref[:, start : start + head_size].astype(jnp.float32)
        scaled = x * lax.rsqrt(jnp.mean(x * x, axis=-1, keepdims=True) + EPS) * gain_ref[...]
        lower, upper = scaled[:, :half], scaled[:, half:]
        out_ref[:, start : start + half] = (lower * cosine - upper * sine).astype(out_ref.dtype)
        out_ref[:, start + half : start + head_size] = (upper * cosine + lower * sine).astype(
            out_ref.dtype
        )


def norm_rope_back(raw_ref, grad_ref, out_ref, gain_ref, cosine, sine):
    head_size = gain_ref.shape[1]
    half = head_size // 2
    gain_grad = jnp.zeros((1, head_size), jnp.float32)
    for start in range(0, raw_ref.shape[1], head_size):
        x = raw_ref[:, start : start + head_size].astype(jnp.float32)
        inverse = lax.rsqrt(jnp.mean(x * x, axis=-1, keepdims=True) + EPS)
        normed = x * inverse
        lower = grad_ref[:, start : start + half]
        upper = grad_ref[:, start + half : start + head_size]
        d_scaled = jnp.concatenate(
            [lower * cosine + upper * sine, upper * cosine - lower * sine], axis=-1
        )
        gain_grad = gain_grad + jnp.sum(d_scaled * normed, axis=0, keepdims=True)
        d_normed = d_scaled * gain_ref[...]
        along = jnp.mean(d_normed * normed, axis=-1, keepdims=True)
        out_ref[:, start : start + head_size] = (inverse * (d_normed - normed * along)).astype(
            out_ref.dtype
        )
    return gain_grad


def greet_signals(barrier, seq, count):
    pl.semaphore_signal(barrier, inc=1, device_id={"seq": other_core(seq)}, device_id_type=MESH)

    @pl.when(seq >= 2)
    def _():
        pl.semaphore_signal(barrier, inc=1, device_id={"seq": seq - 2}, device_id_type=MESH)

    @pl.when(seq + 2 < count)
    def _():
        pl.semaphore_signal(barrier, inc=1, device_id={"seq": seq + 2}, device_id_type=MESH)


def greet_waits(barrier, seq, count, others):
    inside = (seq >= 2) & (seq + 2 < count)

    @pl.when(inside)
    def _():
        pl.semaphore_wait(barrier, others + 3)

    @pl.when(jnp.logical_not(inside))
    def _():
        pl.semaphore_wait(barrier, others + 2)


def other_core(seq):
    return seq + 1 - 2 * lax.rem(seq, 2)


def halo_kernel(
    count, q_ref, k_ref, v_ref, q_gain_ref, k_gain_ref, cos_ref, sin_ref,
    q_out, k_out, v_out, send_sem, recv_sem, copy_sem,
):
    seq = lax.axis_index("seq")
    core = lax.rem(seq, 2)
    cosine, sine = cos_ref[...], sin_ref[...]
    outs = (v_out, k_out)

    def send(which, source, target, hop, device):
        return pltpu.make_async_remote_copy(
            src_ref=outs[which].at[source],
            dst_ref=outs[which].at[target],
            send_sem=send_sem.at[which, hop],
            recv_sem=recv_sem.at[which, hop],
            device_id={"seq": device},
            device_id_type=MESH,
        )

    ahead = seq + 2
    beside = other_core(seq)
    local = pltpu.make_async_copy(v_ref, v_out.at[4], copy_sem)
    local.start()
    barrier = pltpu.get_barrier_semaphore()
    greet_signals(barrier, seq, count)
    greet_waits(barrier, seq, count, 0)
    local.wait()

    def send_own(which):
        @pl.when(ahead < count)
        def _():
            send(which, 4, 2, 0, ahead).start()

    send_own(0)
    norm_rope(k_ref, k_out.at[4], k_gain_ref, cosine, sine)
    send_own(1)
    for which in range(2):

        @pl.when(core == 0)
        def _():
            send(which, 4, 3, 2, beside).start()

        @pl.when(seq < 4)
        def _():
            outs[which][0] = jnp.zeros(outs[which].shape[1:], outs[which].dtype)

        @pl.when(seq < 3)
        def _():
            outs[which][1] = jnp.zeros(outs[which].shape[1:], outs[which].dtype)

        @pl.when(seq < 2)
        def _():
            outs[which][2] = jnp.zeros(outs[which].shape[1:], outs[which].dtype)

        @pl.when(seq < 1)
        def _():
            outs[which][3] = jnp.zeros(outs[which].shape[1:], outs[which].dtype)

    norm_rope(q_ref, q_out, q_gain_ref, cosine, sine)
    for which in range(2):

        @pl.when(seq >= 2)
        def _():
            send(which, 4, 2, 0, ahead).wait_recv()

            @pl.when(ahead < count)
            def _():
                send(which, 2, 0, 1, ahead).start()

            @pl.when(core == 0)
            def _():
                send(which, 2, 1, 3, beside).start()

            @pl.when(core == 1)
            def _():
                send(which, 2, 3, 2, beside).start()

    for which in range(2):

        @pl.when(seq >= 4)
        def _():
            send(which, 2, 0, 1, ahead).wait_recv()

            @pl.when(core == 1)
            def _():
                send(which, 0, 1, 3, beside).start()

    for which in range(2):

        @pl.when(seq >= 1)
        def _():
            send(which, 4, 3, 2, beside).wait_recv()

        @pl.when(seq >= 3)
        def _():
            send(which, 2, 1, 3, beside).wait_recv()

        @pl.when(ahead < count)
        def _():
            send(which, 4, 2, 0, ahead).wait_send()

            @pl.when(seq >= 2)
            def _():
                send(which, 2, 0, 1, ahead).wait_send()

        @pl.when((core == 0) | (seq >= 2))
        def _():
            send(which, 4, 3, 2, beside).wait_send()

        @pl.when(seq >= 2 + 2 * core)
        def _():
            send(which, 2, 1, 3, beside).wait_send()


def attention_group(group, q_ref, keys_ref, vals_ref, do_ref, dq_ref, terms, owns):
    count, rows, columns = keys_ref.shape
    head_size = columns // 2
    span = count * rows
    scale = head_size ** (-0.5)
    lanes = slice(group * head_size, (group + 1) * head_size)
    first_pos = lax.axis_index("seq") * rows
    row = lax.broadcasted_iota(jnp.int32, (rows, span), 0)
    key = lax.broadcasted_iota(jnp.int32, (rows, span), 1)
    visible = (key > row) & (key <= row + WINDOW) & (key >= WINDOW - first_pos)
    across = (((1,), (1,)), ((), ()))
    down = (((0,), (0,)), ((), ()))
    keys = keys_ref[:, :, lanes].reshape(span, head_size)
    vals = vals_ref[:, :, lanes].reshape(span, head_size)
    sums = None
    for head in (2 * group, 2 * group + 1):
        cols = slice(head * head_size, (head + 1) * head_size)
        q, do = q_ref[:, cols], do_ref[:, cols]
        scores = lax.dot_general(q, keys, across, preferred_element_type=jnp.float32)
        scores = jnp.where(visible, scores * scale, MASKED)
        top = jnp.max(scores, axis=-1, keepdims=True)
        powers = jnp.exp(scores - top)
        weights = powers * (1.0 / jnp.sum(powers, axis=-1, keepdims=True))
        dweights = lax.dot_general(do, vals, across, preferred_element_type=jnp.float32)
        delta = jnp.sum(weights * dweights, axis=-1, keepdims=True)
        dscores = (weights * (dweights - delta) * scale).astype(jnp.bfloat16)
        dq_ref[:, cols] = jnp.dot(dscores, keys, preferred_element_type=jnp.float32)
        grads = (
            lax.dot_general(dscores, q, down, preferred_element_type=jnp.float32),
            lax.dot_general(
                weights.astype(jnp.bfloat16), do, down, preferred_element_type=jnp.float32
            ),
        )
        sums = grads if sums is None else tuple(x + y for x, y in zip(sums, grads))
    for which in range(2):
        behind = sums[which][:WINDOW].reshape(count - 1, rows, head_size)
        terms[which, :, :, lanes] = behind.astype(jnp.bfloat16)
        owns[which, :, lanes] = sums[which][WINDOW:]


def key_gain_grad(keys_ref, terms, owns, cosine, sine, turn_ref, gain_ref):
    count, rows, columns = keys_ref.shape
    head_size = columns // 2
    half = head_size // 2
    twice_cos = cosine * cosine - sine * sine
    twice_sin = 2.0 * cosine * sine
    same = jnp.zeros((1, half), jnp.float32)
    turned = jnp.zeros((1, half), jnp.float32)
    for block in range(count):
        real = jnp.zeros((1, half), jnp.float32)
        imag = jnp.zeros((1, half), jnp.float32)
        for start in (0, head_size):
            lower, upper = slice(start, start + half), slice(start + half, start + head_size)
            if block < count - 1:
                a_low = terms[0, block, :, lower].astype(jnp.float32)
                a_up = terms[0, block, :, upper].astype(jnp.float32)
            else:
                a_low, a_up = owns[0, :, lower], owns[0, :, upper]
            b_low = keys_ref[block, :, lower].astype(jnp.float32)
            b_up = keys_ref[block, :, upper].astype(jnp.float32)
            low, up = a_low * b_low, a_up * b_up
            x, y = low - up, a_low * b_up + a_up * b_low
            same = same + jnp.sum(low + up, axis=0, keepdims=True)
            real = real + jnp.sum(x * twice_cos + y * twice_sin, axis=0, keepdims=True)
            imag = imag + jnp.sum(y * twice_cos - x * twice_sin, axis=0, keepdims=True)
        turned = (
            turned
            + real * turn_ref[block : block + 1, :half]
            - imag * turn_ref[block : block + 1, half:]
        )
    grad = jnp.concatenate([same + turned, same - turned], axis=-1) * 0.5
    return grad / gain_ref[...]


def backward_kernel(
    seq_size, dp_size, q_rot_ref, keys_ref, vals_ref, do_ref, q_ref, k_ref, q_gain_ref, k_gain_ref,
    cos_ref, sin_ref, turn_ref, q_out, k_out, v_out, q_gain_out, k_gain_out,
    dq_ref, terms, owns, beside_buf, behind_buf, sent_buf, send_sem, recv_sem,
    x_ref, slots_a, slots_b, slots_c, part_b, part_c, gain_send_sem, gain_recv_sem,
):
    seq = lax.axis_index("seq")
    dp = lax.axis_index("dp")
    core = lax.rem(seq, 2)
    behind = seq - 2
    beside = other_core(seq)
    cosine, sine = cos_ref[...], sin_ref[...]

    z_lo_size = seq_size // LOW
    z_size = z_lo_size * (dp_size // X_SIZE)
    low = lax.rem(seq, LOW)
    z_lo = lax.div(seq, LOW)
    x_pos = lax.rem(dp, X_SIZE)
    z_pos = lax.div(dp, X_SIZE) * z_lo_size + z_lo

    def peer_a(k):
        return {"seq": z_lo * LOW + lax.rem(low + k, LOW), "dp": dp}

    def peer_b(k):
        return {"seq": seq, "dp": dp - x_pos + lax.rem(x_pos + k, X_SIZE)}

    def peer_c(k):
        z_other = lax.rem(z_pos + k, z_size)
        return {
            "seq": lax.rem(z_other, z_lo_size) * LOW + low,
            "dp": lax.div(z_other, z_lo_size) * X_SIZE + x_pos,
        }

    stages = ((z_size, peer_c, z_pos), (LOW, peer_a, low), (X_SIZE, peer_b, x_pos))
    barrier = pltpu.get_barrier_semaphore()
    greeted = 0
    for size, peer, _ in stages:
        for k in range(1, size):
            pl.semaphore_signal(barrier, inc=1, device_id=peer(k), device_id_type=MESH)
            greeted += 1
    greet_signals(barrier, seq, seq_size)
    heads = (q_rot_ref, keys_ref, vals_ref, do_ref, dq_ref, terms, owns)
    attention_group(0, *heads)
    attention_group(1, *heads)
    greet_waits(barrier, seq, seq_size, greeted)

    def swap(which, part):
        return pltpu.make_async_remote_copy(
            src_ref=terms.at[which, 3 - 2 * part],
            dst_ref=beside_buf.at[which, part],
            send_sem=send_sem.at[which, part],
            recv_sem=recv_sem.at[which, part],
            device_id={"seq": beside},
            device_id_type=MESH,
        )

    def hop(which, part):
        return pltpu.make_async_remote_copy(
            src_ref=sent_buf.at[which, part],
            dst_ref=behind_buf.at[which, part],
            send_sem=send_sem.at[which, 2 + part],
            recv_sem=recv_sem.at[which, 2 + part],
            device_id={"seq": behind},
            device_id_type=MESH,
        )

    sources = (x_ref, part_b, part_c)
    results = (part_b, part_c, x_ref)
    slot_refs = (slots_c, slots_a, slots_b)
    bases = (0, z_size - 1, z_size + LOW - 2)

    def gain_copies(stage):
        size, peer, _ = stages[stage]
        return [
            pltpu.make_async_remote_copy(
                src_ref=sources[stage],
                dst_ref=slot_refs[stage].at[k],
                send_sem=gain_send_sem.at[bases[stage] + k - 1],
                recv_sem=gain_recv_sem.at[bases[stage] + k - 1],
                device_id=peer(k),
                device_id_type=MESH,
            )
            for k in range(1, size)
        ]

    def gain_start(stage):
        for copy in gain_copies(stage):
            copy.start()
        slot_refs[stage][0] = sources[stage][...]

    def gain_end(stage):
        for copy in gain_copies(stage):
            copy.wait()
        size, _, mine = stages[stage]
        slots = slot_refs[stage]
        acc = slots[lax.rem(mine + size, size)]
        for j in range(1, size):
            acc = acc + slots[lax.rem(mine - j + size, size)]
        results[stage][...] = acc

    for which in range(2):
        swap(which, 1).start()
    for which in range(2):
        swap(which, 0).start()
    for which in range(2):
        swap(which, 1).wait()
        four = terms[which, 0]

        @pl.when(core == 0)
        def _():
            sent_buf[which, 0] = four

        @pl.when(core == 1)
        def _():
            sent_buf[which, 0] = (
                four.astype(jnp.float32) + beside_buf[which, 1].astype(jnp.float32)
            ).astype(jnp.bfloat16)

        @pl.when(seq >= 2)
        def _():
            hop(which, 0).start()

    k_gain = key_gain_grad(keys_ref, terms, owns, cosine, sine, turn_ref, k_gain_ref)
    q_gain = norm_rope_back(q_ref, dq_ref, q_out, q_gain_ref, cosine, sine)
    half = q_gain.shape[1] // 2
    x_ref[...] = jnp.zeros_like(x_ref)
    x_ref[0:1, :] = q_gain[:, :half]
    x_ref[1:2, :] = q_gain[:, half:]
    x_ref[2:3, :] = k_gain[:, :half]
    x_ref[3:4, :] = k_gain[:, half:]
    gain_start(0)
    for which in range(2):
        swap(which, 0).wait()
        two = terms[which, 2].astype(jnp.float32) + beside_buf[which, 1 - core].astype(jnp.float32)

        @pl.when(seq + 2 < seq_size)
        def _():
            hop(which, 0).wait_recv()
            sent_buf[which, 1] = (two + behind_buf[which, 0].astype(jnp.float32)).astype(
                jnp.bfloat16
            )

        @pl.when(seq + 2 >= seq_size)
        def _():
            sent_buf[which, 1] = two.astype(jnp.bfloat16)

        @pl.when(seq >= 2)
        def _():
            hop(which, 1).start()

        gain_end(which)
        gain_start(which + 1)

    for which in range(2):

        @pl.when(seq + 2 < seq_size)
        def _():
            hop(which, 1).wait_recv()
            owns[which] = owns[which] + behind_buf[which, 1].astype(jnp.float32)

        @pl.when(core == 0)
        def _():
            owns[which] = owns[which] + beside_buf[which, 0].astype(jnp.float32)

        if which == 0:
            norm_rope_back(k_ref, owns.at[0], k_out, k_gain_ref, cosine, sine)

    v_out[...] = owns[1].astype(v_out.dtype)
    gain_end(2)
    for out, start in ((q_gain_out, 0), (k_gain_out, 2)):
        out[:, :half] = x_ref[start : start + 1, :]
        out[:, half:] = x_ref[start + 1 : start + 2, :]
    for which in range(2):

        @pl.when(seq >= 2)
        def _():
            hop(which, 0).wait_send()
            hop(which, 1).wait_send()


VMEM_SPEC = pl.BlockSpec(memory_space=pltpu.VMEM)


def halo(seq_size, *args):
    q, k = args[0], args[1]
    return pl.pallas_call(
        lambda *refs: halo_kernel(seq_size, *refs),
        out_shape=(
            jax.ShapeDtypeStruct(q.shape, jnp.bfloat16),
            jax.ShapeDtypeStruct((5,) + k.shape, jnp.bfloat16),
            jax.ShapeDtypeStruct((5,) + k.shape, jnp.bfloat16),
        ),
        in_specs=[VMEM_SPEC] * 7,
        out_specs=(VMEM_SPEC,) * 3,
        scratch_shapes=[
            pltpu.SemaphoreType.DMA((2, 4)),
            pltpu.SemaphoreType.DMA((2, 4)),
            pltpu.SemaphoreType.DMA,
        ],
        compiler_params=pltpu.CompilerParams(collective_id=1, has_side_effects=True),
        name="halo",
    )(*args)


def backward(seq_size, dp_size, *args):
    q, keys, k = args[0], args[1], args[5]
    rows, columns = k.shape
    head_size = columns // 2
    z_size = seq_size // LOW * (dp_size // X_SIZE)
    peers = LOW + X_SIZE + z_size - 3
    gains = (8, 128)
    return pl.pallas_call(
        lambda *refs: backward_kernel(seq_size, dp_size, *refs),
        out_shape=(
            jax.ShapeDtypeStruct(q.shape, jnp.bfloat16),
            jax.ShapeDtypeStruct(k.shape, jnp.bfloat16),
            jax.ShapeDtypeStruct(k.shape, jnp.bfloat16),
            jax.ShapeDtypeStruct((1, head_size), jnp.float32),
            jax.ShapeDtypeStruct((1, head_size), jnp.float32),
        ),
        in_specs=[VMEM_SPEC] * 11,
        out_specs=(VMEM_SPEC,) * 5,
        scratch_shapes=[
            pltpu.VMEM(q.shape, jnp.float32),
            pltpu.VMEM((2, keys.shape[0] - 1, rows, columns), jnp.bfloat16),
            pltpu.VMEM((2, rows, columns), jnp.float32),
            pltpu.VMEM((2, 2, rows, columns), jnp.bfloat16),
            pltpu.VMEM((2, 2, rows, columns), jnp.bfloat16),
            pltpu.VMEM((2, 2, rows, columns), jnp.bfloat16),
            pltpu.SemaphoreType.DMA((2, 4)),
            pltpu.SemaphoreType.DMA((2, 4)),
            pltpu.VMEM(gains, jnp.float32),
            pltpu.VMEM((LOW,) + gains, jnp.float32),
            pltpu.VMEM((X_SIZE,) + gains, jnp.float32),
            pltpu.VMEM((z_size,) + gains, jnp.float32),
            pltpu.VMEM(gains, jnp.float32),
            pltpu.VMEM(gains, jnp.float32),
            pltpu.SemaphoreType.DMA((peers,)),
            pltpu.SemaphoreType.DMA((peers,)),
        ],
        compiler_params=pltpu.CompilerParams(collective_id=0, has_side_effects=True),
        name="backward",
    )(*args)


def hand_out_kernel(*refs):
    half = len(refs) // 2
    for source, target in zip(refs[:half], refs[half:]):
        target[...] = source[...]


def hand_out(*results):
    return pl.pallas_call(
        hand_out_kernel,
        out_shape=tuple(jax.ShapeDtypeStruct(r.shape, r.dtype) for r in results),
        in_specs=[VMEM_SPEC] * len(results),
        out_specs=(VMEM_SPEC,) * len(results),
        name="hand_out",
    )(*results)


def local(seq_size, dp_size, q_raw, k_raw, values, grad_out, q_gain, k_gain):
    q_local, k_local, v_local, do_local = q_raw[0], k_raw[0], values[0], grad_out[0]
    rows = k_local.shape[0]
    head_size = q_gain.shape[0]
    positions = lax.axis_index("seq") * rows + jnp.arange(rows, dtype=jnp.int32)
    cosine, sine = rope_tables(positions, head_size)
    back = np.maximum(4 - np.arange(8), 0)[:, None] * (2.0 * rows)
    angles = back * ROPE_BASE ** (-2.0 * np.arange(head_size // 2) / head_size)
    turn = jnp.asarray(np.concatenate([np.cos(angles), np.sin(angles)], -1), jnp.float32)
    q_gain, k_gain = q_gain[None], k_gain[None]
    q_rot, keys, vals = halo(seq_size, q_local, k_local, v_local, q_gain, k_gain, cosine, sine)
    grad_q, grad_k, grad_v, grad_q_gain, grad_k_gain = backward(
        seq_size, dp_size, q_rot, keys, vals, do_local, q_local, k_local, q_gain, k_gain,
        cosine, sine, turn,
    )
    grad_q, grad_k, grad_v, grad_q_gain, grad_k_gain = hand_out(
        grad_q, grad_k, grad_v, grad_q_gain, grad_k_gain
    )
    return (grad_q[None], grad_k[None], grad_v[None], grad_q_gain[0], grad_k_gain[0])


def solution(mesh):
    return jax.shard_map(
        lambda *args: local(mesh.shape["seq"], mesh.shape["dp"], *args),
        mesh=mesh,
        in_specs=(
            P("dp", "seq", None),
            P("dp", "seq", None),
            P("dp", "seq", None),
            P("dp", "seq", None),
            P(),
            P(),
        ),
        out_specs=(P("dp", "seq", None), P("dp", "seq", None), P("dp", "seq", None), P(), P()),
        check_vma=False,
    )
```

```python
import jax
import jax.numpy as jnp
import numpy as np
from jax import lax
from jax.experimental import pallas as pl
from jax.experimental.pallas import tpu as pltpu
from jax.sharding import PartitionSpec as P

WINDOW = 1024


EPS = 1e-06
ROPE_BASE = 10000.0
MASKED = -1e30
MESH = pl.DeviceIdType.MESH

LOW = 8
X_SIZE = 4


def rope_tables(positions, head_size):
    half_size = head_size // 2
    freqs = jnp.power(ROPE_BASE, -(2.0 * jnp.arange(half_size, dtype=jnp.float32)) / head_size)
    angles = positions.astype(jnp.float32)[:, None] * freqs[None, :]
    return (jnp.cos(angles), jnp.sin(angles))


def norm_rope(raw_ref, out_ref, gain_ref, cosine, sine):
    head_size = gain_ref.shape[1]
    half = head_size // 2
    for start in range(0, raw_ref.shape[1], head_size):
        x = raw_ref[:, start : start + head_size].astype(jnp.float32)
        scaled = x * lax.rsqrt(jnp.mean(x * x, axis=-1, keepdims=True) + EPS) * gain_ref[...]
        lower, upper = scaled[:, :half], scaled[:, half:]
        out_ref[:, start : start + half] = (lower * cosine - upper * sine).astype(out_ref.dtype)
        out_ref[:, start + half : start + head_size] = (upper * cosine + lower * sine).astype(
            out_ref.dtype
        )


def norm_rope_back(raw_ref, grad_ref, out_ref, gain_ref, cosine, sine):
    head_size = gain_ref.shape[1]
    half = head_size // 2
    gain_grad = jnp.zeros((1, head_size), jnp.float32)
    for start in range(0, raw_ref.shape[1], head_size):
        x = raw_ref[:, start : start + head_size].astype(jnp.float32)
        inverse = lax.rsqrt(jnp.mean(x * x, axis=-1, keepdims=True) + EPS)
        normed = x * inverse
        lower = grad_ref[:, start : start + half]
        upper = grad_ref[:, start + half : start + head_size]
        d_scaled = jnp.concatenate(
            [lower * cosine + upper * sine, upper * cosine - lower * sine], axis=-1
        )
        gain_grad = gain_grad + jnp.sum(d_scaled * normed, axis=0, keepdims=True)
        d_normed = d_scaled * gain_ref[...]
        along = jnp.mean(d_normed * normed, axis=-1, keepdims=True)
        out_ref[:, start : start + head_size] = (inverse * (d_normed - normed * along)).astype(
            out_ref.dtype
        )
    return gain_grad


def greet_signals(barrier, seq, count):
    pl.semaphore_signal(barrier, inc=1, device_id={"seq": other_core(seq)}, device_id_type=MESH)

    @pl.when(seq >= 2)
    def _():
        pl.semaphore_signal(barrier, inc=1, device_id={"seq": seq - 2}, device_id_type=MESH)

    @pl.when(seq + 2 < count)
    def _():
        pl.semaphore_signal(barrier, inc=1, device_id={"seq": seq + 2}, device_id_type=MESH)


def greet_waits(barrier, seq, count, others):
    inside = (seq >= 2) & (seq + 2 < count)

    @pl.when(inside)
    def _():
        pl.semaphore_wait(barrier, others + 3)

    @pl.when(jnp.logical_not(inside))
    def _():
        pl.semaphore_wait(barrier, others + 2)


def other_core(seq):
    return seq + 1 - 2 * lax.rem(seq, 2)


def halo_kernel(
    count, q_ref, k_ref, v_ref, q_gain_ref, k_gain_ref, cos_ref, sin_ref,
    q_out, k_out, v_out, send_sem, recv_sem, copy_sem,
):
    seq = lax.axis_index("seq")
    core = lax.rem(seq, 2)
    cosine, sine = cos_ref[...], sin_ref[...]
    outs = (v_out, k_out)

    def send(which, source, target, hop, device):
        return pltpu.make_async_remote_copy(
            src_ref=outs[which].at[source],
            dst_ref=outs[which].at[target],
            send_sem=send_sem.at[which, hop],
            recv_sem=recv_sem.at[which, hop],
            device_id={"seq": device},
            device_id_type=MESH,
        )

    ahead = seq + 2
    beside = other_core(seq)
    local = pltpu.make_async_copy(v_ref, v_out.at[4], copy_sem)
    local.start()
    barrier = pltpu.get_barrier_semaphore()
    greet_signals(barrier, seq, count)
    greet_waits(barrier, seq, count, 0)
    local.wait()

    def send_own(which):
        @pl.when(ahead < count)
        def _():
            send(which, 4, 2, 0, ahead).start()

    send_own(0)
    norm_rope(k_ref, k_out.at[4], k_gain_ref, cosine, sine)
    send_own(1)
    for which in range(2):

        @pl.when(core == 0)
        def _():
            send(which, 4, 3, 2, beside).start()

        @pl.when(seq < 4)
        def _():
            outs[which][0] = jnp.zeros(outs[which].shape[1:], outs[which].dtype)

        @pl.when(seq < 3)
        def _():
            outs[which][1] = jnp.zeros(outs[which].shape[1:], outs[which].dtype)

        @pl.when(seq < 2)
        def _():
            outs[which][2] = jnp.zeros(outs[which].shape[1:], outs[which].dtype)

        @pl.when(seq < 1)
        def _():
            outs[which][3] = jnp.zeros(outs[which].shape[1:], outs[which].dtype)

    norm_rope(q_ref, q_out, q_gain_ref, cosine, sine)
    for which in range(2):

        @pl.when(seq >= 2)
        def _():
            send(which, 4, 2, 0, ahead).wait_recv()

            @pl.when(ahead < count)
            def _():
                send(which, 2, 0, 1, ahead).start()

            @pl.when(core == 0)
            def _():
                send(which, 2, 1, 3, beside).start()

            @pl.when(core == 1)
            def _():
                send(which, 2, 3, 2, beside).start()

    for which in range(2):

        @pl.when(seq >= 4)
        def _():
            send(which, 2, 0, 1, ahead).wait_recv()

            @pl.when(core == 1)
            def _():
                send(which, 0, 1, 3, beside).start()

    for which in range(2):

        @pl.when(seq >= 1)
        def _():
            send(which, 4, 3, 2, beside).wait_recv()

        @pl.when(seq >= 3)
        def _():
            send(which, 2, 1, 3, beside).wait_recv()

        @pl.when(ahead < count)
        def _():
            send(which, 4, 2, 0, ahead).wait_send()

            @pl.when(seq >= 2)
            def _():
                send(which, 2, 0, 1, ahead).wait_send()

        @pl.when((core == 0) | (seq >= 2))
        def _():
            send(which, 4, 3, 2, beside).wait_send()

        @pl.when(seq >= 2 + 2 * core)
        def _():
            send(which, 2, 1, 3, beside).wait_send()


def attention_group(group, q_ref, keys_ref, vals_ref, do_ref, dq_ref, terms, owns):
    count, rows, columns = keys_ref.shape
    head_size = columns // 2
    span = count * rows
    scale = head_size ** (-0.5)
    lanes = slice(group * head_size, (group + 1) * head_size)
    first_pos = lax.axis_index("seq") * rows
    row = lax.broadcasted_iota(jnp.int32, (rows, span), 0)
    key = lax.broadcasted_iota(jnp.int32, (rows, span), 1)
    visible = (key > row) & (key <= row + WINDOW) & (key >= WINDOW - first_pos)
    across = (((1,), (1,)), ((), ()))
    down = (((0,), (0,)), ((), ()))
    keys = keys_ref[:, :, lanes].reshape(span, head_size)
    vals = vals_ref[:, :, lanes].reshape(span, head_size)
    sums = None
    for head in (2 * group, 2 * group + 1):
        cols = slice(head * head_size, (head + 1) * head_size)
        q, do = q_ref[:, cols], do_ref[:, cols]
        scores = lax.dot_general(q, keys, across, preferred_element_type=jnp.float32)
        scores = jnp.where(visible, scores * scale, MASKED)
        top = jnp.max(scores, axis=-1, keepdims=True)
        powers = jnp.exp(scores - top)
        weights = powers * (1.0 / jnp.sum(powers, axis=-1, keepdims=True))
        dweights = lax.dot_general(do, vals, across, preferred_element_type=jnp.float32)
        delta = jnp.sum(weights * dweights, axis=-1, keepdims=True)
        dscores = (weights * (dweights - delta) * scale).astype(jnp.bfloat16)
        dq_ref[:, cols] = jnp.dot(dscores, keys, preferred_element_type=jnp.float32)
        grads = (
            lax.dot_general(dscores, q, down, preferred_element_type=jnp.float32),
            lax.dot_general(
                weights.astype(jnp.bfloat16), do, down, preferred_element_type=jnp.float32
            ),
        )
        sums = grads if sums is None else tuple(x + y for x, y in zip(sums, grads))
    for which in range(2):
        behind = sums[which][:WINDOW].reshape(count - 1, rows, head_size)
        terms[which, :, :, lanes] = behind.astype(jnp.bfloat16)
        owns[which, :, lanes] = sums[which][WINDOW:]


def key_gain_grad(keys_ref, terms, owns, cosine, sine, turn_ref, gain_ref):
    count, rows, columns = keys_ref.shape
    head_size = columns // 2
    half = head_size // 2
    twice_cos = cosine * cosine - sine * sine
    twice_sin = 2.0 * cosine * sine
    same = jnp.zeros((1, half), jnp.float32)
    turned = jnp.zeros((1, half), jnp.float32)
    for block in range(count):
        real = jnp.zeros((1, half), jnp.float32)
        imag = jnp.zeros((1, half), jnp.float32)
        for start in (0, head_size):
            lower, upper = slice(start, start + half), slice(start + half, start + head_size)
            if block < count - 1:
                a_low = terms[0, block, :, lower].astype(jnp.float32)
                a_up = terms[0, block, :, upper].astype(jnp.float32)
            else:
                a_low, a_up = owns[0, :, lower], owns[0, :, upper]
            b_low = keys_ref[block, :, lower].astype(jnp.float32)
            b_up = keys_ref[block, :, upper].astype(jnp.float32)
            low, up = a_low * b_low, a_up * b_up
            x, y = low - up, a_low * b_up + a_up * b_low
            same = same + jnp.sum(low + up, axis=0, keepdims=True)
            real = real + jnp.sum(x * twice_cos + y * twice_sin, axis=0, keepdims=True)
            imag = imag + jnp.sum(y * twice_cos - x * twice_sin, axis=0, keepdims=True)
        turned = (
            turned
            + real * turn_ref[block : block + 1, :half]
            - imag * turn_ref[block : block + 1, half:]
        )
    grad = jnp.concatenate([same + turned, same - turned], axis=-1) * 0.5
    return grad / gain_ref[...]


def backward_kernel(
    seq_size, dp_size, q_rot_ref, keys_ref, vals_ref, do_ref, q_ref, k_ref, q_gain_ref, k_gain_ref,
    cos_ref, sin_ref, turn_ref, q_out, k_out, v_out, q_gain_out, k_gain_out,
    dq_ref, terms, owns, beside_buf, behind_buf, sent_buf, send_sem, recv_sem,
    x_ref, slots_a, slots_b, slots_c, part_b, part_c, gain_send_sem, gain_recv_sem,
):
    seq = lax.axis_index("seq")
    dp = lax.axis_index("dp")
    core = lax.rem(seq, 2)
    behind = seq - 2
    beside = other_core(seq)
    cosine, sine = cos_ref[...], sin_ref[...]

    z_lo_size = seq_size // LOW
    z_size = z_lo_size * (dp_size // X_SIZE)
    low = lax.rem(seq, LOW)
    z_lo = lax.div(seq, LOW)
    x_pos = lax.rem(dp, X_SIZE)
    z_pos = lax.div(dp, X_SIZE) * z_lo_size + z_lo

    def peer_a(k):
        return {"seq": z_lo * LOW + lax.rem(low + k, LOW), "dp": dp}

    def peer_b(k):
        return {"seq": seq, "dp": dp - x_pos + lax.rem(x_pos + k, X_SIZE)}

    def peer_c(k):
        z_other = lax.rem(z_pos + k, z_size)
        return {
            "seq": lax.rem(z_other, z_lo_size) * LOW + low,
            "dp": lax.div(z_other, z_lo_size) * X_SIZE + x_pos,
        }

    stages = ((z_size, peer_c, z_pos), (X_SIZE, peer_b, x_pos), (LOW, peer_a, low))
    barrier = pltpu.get_barrier_semaphore()
    greeted = 0
    for size, peer, _ in stages:
        for k in range(1, size):
            pl.semaphore_signal(barrier, inc=1, device_id=peer(k), device_id_type=MESH)
            greeted += 1
    greet_signals(barrier, seq, seq_size)
    heads = (q_rot_ref, keys_ref, vals_ref, do_ref, dq_ref, terms, owns)
    attention_group(0, *heads)
    attention_group(1, *heads)
    greet_waits(barrier, seq, seq_size, greeted)

    def swap(which, part):
        return pltpu.make_async_remote_copy(
            src_ref=terms.at[which, 3 - 2 * part],
            dst_ref=beside_buf.at[which, part],
            send_sem=send_sem.at[which, part],
            recv_sem=recv_sem.at[which, part],
            device_id={"seq": beside},
            device_id_type=MESH,
        )

    def hop(which, part):
        return pltpu.make_async_remote_copy(
            src_ref=sent_buf.at[which, part],
            dst_ref=behind_buf.at[which, part],
            send_sem=send_sem.at[which, 2 + part],
            recv_sem=recv_sem.at[which, 2 + part],
            device_id={"seq": behind},
            device_id_type=MESH,
        )

    sources = (x_ref, part_b, part_c)
    results = (part_b, part_c, x_ref)
    slot_refs = (slots_c, slots_b, slots_a)
    bases = (0, z_size - 1, z_size + X_SIZE - 2)

    def gain_copies(stage):
        size, peer, _ = stages[stage]
        return [
            pltpu.make_async_remote_copy(
                src_ref=sources[stage],
                dst_ref=slot_refs[stage].at[k],
                send_sem=gain_send_sem.at[bases[stage] + k - 1],
                recv_sem=gain_recv_sem.at[bases[stage] + k - 1],
                device_id=peer(k),
                device_id_type=MESH,
            )
            for k in range(1, size)
        ]

    def gain_start(stage):
        for copy in gain_copies(stage):
            copy.start()
        slot_refs[stage][0] = sources[stage][...]

    def gain_end(stage):
        for copy in gain_copies(stage):
            copy.wait()
        size, _, mine = stages[stage]
        slots = slot_refs[stage]
        acc = slots[lax.rem(mine + size, size)]
        for j in range(1, size):
            acc = acc + slots[lax.rem(mine - j + size, size)]
        results[stage][...] = acc

    for which in range(2):
        swap(which, 1).start()
    for which in range(2):
        swap(which, 0).start()
    for which in range(2):
        swap(which, 1).wait()
        four = terms[which, 0]

        @pl.when(core == 0)
        def _():
            sent_buf[which, 0] = four

        @pl.when(core == 1)
        def _():
            sent_buf[which, 0] = (
                four.astype(jnp.float32) + beside_buf[which, 1].astype(jnp.float32)
            ).astype(jnp.bfloat16)

        @pl.when(seq >= 2)
        def _():
            hop(which, 0).start()

    k_gain = key_gain_grad(keys_ref, terms, owns, cosine, sine, turn_ref, k_gain_ref)
    q_gain = norm_rope_back(q_ref, dq_ref, q_out, q_gain_ref, cosine, sine)
    half = q_gain.shape[1] // 2
    x_ref[...] = jnp.zeros_like(x_ref)
    x_ref[0:1, :] = q_gain[:, :half]
    x_ref[1:2, :] = q_gain[:, half:]
    x_ref[2:3, :] = k_gain[:, :half]
    x_ref[3:4, :] = k_gain[:, half:]
    gain_start(0)
    for which in range(2):
        swap(which, 0).wait()
        two = terms[which, 2].astype(jnp.float32) + beside_buf[which, 1 - core].astype(jnp.float32)

        @pl.when(seq + 2 < seq_size)
        def _():
            hop(which, 0).wait_recv()
            sent_buf[which, 1] = (two + behind_buf[which, 0].astype(jnp.float32)).astype(
                jnp.bfloat16
            )

        @pl.when(seq + 2 >= seq_size)
        def _():
            sent_buf[which, 1] = two.astype(jnp.bfloat16)

        @pl.when(seq >= 2)
        def _():
            hop(which, 1).start()

    for stage in range(2):
        gain_end(stage)
        gain_start(stage + 1)

    for which in range(2):

        @pl.when(seq + 2 < seq_size)
        def _():
            hop(which, 1).wait_recv()
            owns[which] = owns[which] + behind_buf[which, 1].astype(jnp.float32)

        @pl.when(core == 0)
        def _():
            owns[which] = owns[which] + beside_buf[which, 0].astype(jnp.float32)

        if which == 0:
            norm_rope_back(k_ref, owns.at[0], k_out, k_gain_ref, cosine, sine)

    v_out[...] = owns[1].astype(v_out.dtype)
    gain_end(2)
    for out, start in ((q_gain_out, 0), (k_gain_out, 2)):
        out[:, :half] = x_ref[start : start + 1, :]
        out[:, half:] = x_ref[start + 1 : start + 2, :]
    for which in range(2):

        @pl.when(seq >= 2)
        def _():
            hop(which, 0).wait_send()
            hop(which, 1).wait_send()


VMEM_SPEC = pl.BlockSpec(memory_space=pltpu.VMEM)


def halo(seq_size, *args):
    q, k = args[0], args[1]
    return pl.pallas_call(
        lambda *refs: halo_kernel(seq_size, *refs),
        out_shape=(
            jax.ShapeDtypeStruct(q.shape, jnp.bfloat16),
            jax.ShapeDtypeStruct((5,) + k.shape, jnp.bfloat16),
            jax.ShapeDtypeStruct((5,) + k.shape, jnp.bfloat16),
        ),
        in_specs=[VMEM_SPEC] * 7,
        out_specs=(VMEM_SPEC,) * 3,
        scratch_shapes=[
            pltpu.SemaphoreType.DMA((2, 4)),
            pltpu.SemaphoreType.DMA((2, 4)),
            pltpu.SemaphoreType.DMA,
        ],
        compiler_params=pltpu.CompilerParams(collective_id=1, has_side_effects=True),
        name="halo",
    )(*args)


def backward(seq_size, dp_size, *args):
    q, keys, k = args[0], args[1], args[5]
    rows, columns = k.shape
    head_size = columns // 2
    z_size = seq_size // LOW * (dp_size // X_SIZE)
    peers = LOW + X_SIZE + z_size - 3
    gains = (8, 128)
    return pl.pallas_call(
        lambda *refs: backward_kernel(seq_size, dp_size, *refs),
        out_shape=(
            jax.ShapeDtypeStruct(q.shape, jnp.bfloat16),
            jax.ShapeDtypeStruct(k.shape, jnp.bfloat16),
            jax.ShapeDtypeStruct(k.shape, jnp.bfloat16),
            jax.ShapeDtypeStruct((1, head_size), jnp.float32),
            jax.ShapeDtypeStruct((1, head_size), jnp.float32),
        ),
        in_specs=[VMEM_SPEC] * 11,
        out_specs=(VMEM_SPEC,) * 5,
        scratch_shapes=[
            pltpu.VMEM(q.shape, jnp.float32),
            pltpu.VMEM((2, keys.shape[0] - 1, rows, columns), jnp.bfloat16),
            pltpu.VMEM((2, rows, columns), jnp.float32),
            pltpu.VMEM((2, 2, rows, columns), jnp.bfloat16),
            pltpu.VMEM((2, 2, rows, columns), jnp.bfloat16),
            pltpu.VMEM((2, 2, rows, columns), jnp.bfloat16),
            pltpu.SemaphoreType.DMA((2, 4)),
            pltpu.SemaphoreType.DMA((2, 4)),
            pltpu.VMEM(gains, jnp.float32),
            pltpu.VMEM((LOW,) + gains, jnp.float32),
            pltpu.VMEM((X_SIZE,) + gains, jnp.float32),
            pltpu.VMEM((z_size,) + gains, jnp.float32),
            pltpu.VMEM(gains, jnp.float32),
            pltpu.VMEM(gains, jnp.float32),
            pltpu.SemaphoreType.DMA((peers,)),
            pltpu.SemaphoreType.DMA((peers,)),
        ],
        compiler_params=pltpu.CompilerParams(collective_id=0, has_side_effects=True),
        name="backward",
    )(*args)


def hand_out_kernel(*refs):
    half = len(refs) // 2
    for source, target in zip(refs[:half], refs[half:]):
        target[...] = source[...]


def hand_out(*results):
    return pl.pallas_call(
        hand_out_kernel,
        out_shape=tuple(jax.ShapeDtypeStruct(r.shape, r.dtype) for r in results),
        in_specs=[VMEM_SPEC] * len(results),
        out_specs=(VMEM_SPEC,) * len(results),
        name="hand_out",
    )(*results)


def local(seq_size, dp_size, q_raw, k_raw, values, grad_out, q_gain, k_gain):
    q_local, k_local, v_local, do_local = q_raw[0], k_raw[0], values[0], grad_out[0]
    rows = k_local.shape[0]
    head_size = q_gain.shape[0]
    positions = lax.axis_index("seq") * rows + jnp.arange(rows, dtype=jnp.int32)
    cosine, sine = rope_tables(positions, head_size)
    back = np.maximum(4 - np.arange(8), 0)[:, None] * (2.0 * rows)
    angles = back * ROPE_BASE ** (-2.0 * np.arange(head_size // 2) / head_size)
    turn = jnp.asarray(np.concatenate([np.cos(angles), np.sin(angles)], -1), jnp.float32)
    q_gain, k_gain = q_gain[None], k_gain[None]
    q_rot, keys, vals = halo(seq_size, q_local, k_local, v_local, q_gain, k_gain, cosine, sine)
    grad_q, grad_k, grad_v, grad_q_gain, grad_k_gain = backward(
        seq_size, dp_size, q_rot, keys, vals, do_local, q_local, k_local, q_gain, k_gain,
        cosine, sine, turn,
    )
    grad_q, grad_k, grad_v, grad_q_gain, grad_k_gain = hand_out(
        grad_q, grad_k, grad_v, grad_q_gain, grad_k_gain
    )
    return (grad_q[None], grad_k[None], grad_v[None], grad_q_gain[0], grad_k_gain[0])


def solution(mesh):
    return jax.shard_map(
        lambda *args: local(mesh.shape["seq"], mesh.shape["dp"], *args),
        mesh=mesh,
        in_specs=(
            P("dp", "seq", None),
            P("dp", "seq", None),
            P("dp", "seq", None),
            P("dp", "seq", None),
            P(),
            P(),
        ),
        out_specs=(P("dp", "seq", None), P("dp", "seq", None), P("dp", "seq", None), P(), P()),
        check_vma=False,
    )
```
